256 devices in a mesh: space: 64 (over z, x, core), chan: 4 (over y).
Axes of the slice: x: 4, y: 4, z: 8, core: 2. Of those that a mesh axis runs over, the one named last changes fastest.
Arguments:
- features: float32 [256, 32768], P('chan', 'space'), may hold values from -6 to 6
- positions: float32 [3, 32768], P(None, 'space'), may hold values from 0 to 2, as said below
- counts: int32 [128], P('space'), may hold values from 1 to 256, as said below
- neighbours: int32 [128, 4], P('space'), may hold values from 0 to 5, as said below
- wavevectors: int32 [3, 512], replicated, may hold values from -4 to 4, as said below
- filters: float32 [8, 256, 256], P(None, 'chan'), may hold values from -0.125 to 0.125
- cotangent: float32 [256, 32768], P('chan', 'space'), may hold values from -6 to 6
Outputs:
- updated: float32 [256, 32768], P('chan', 'space')
- grad_features: float32 [256, 32768], P('chan', 'space')
The draws below stay inside these ranges and needn't reach their ends.
Inputs may be any that keep to these rules, and one draw needn't show every extreme that they name: `counts`: at least one block holds 256 live atoms. `neighbours`: entry e names block e mod 2 of the previous (e // 2 = 0), the same (1) or the next (2) slab layer, the layers closing into a loop; the first entry of a row is the block itself, the entries of a row differ, and each names a block whose position within its layer differs from the row's by at most one. `wavevectors`: no column is all zeros. `positions`: the first coordinate lies in [0, 1], the second in [b, b + 1] for the b-th block of a layer, the third in [0, 1].
All inputs are finite; a program needn't handle non-finite values.
Results may differ from the reference program's by a relative error of at most 0.0003.
Values sent between devices are 32-bit elements; how exact they have to be, the bound alone decides.
No kernel may reach another device: no remote copies, remote signals or barrier semaphores. Data moves between devices by JAX's collectives and lax.ppermute only.
A program may use at most 64 MiB of HBM per device.

```python
import math
import jax
import jax.numpy as jnp
from jax import lax

C = 256
NRAD = 8
K = 512
NB = 4
CAP = 256
BLK_DEV = 2
BLOCKS = 128
SLOTS = 32768
N_SPACE = 64


def draw_positions(key, part):
    unit = jax.random.uniform(key, (3, SLOTS), jnp.float32)
    slot_index = jnp.arange(SLOTS)
    local_block = (slot_index // CAP % BLK_DEV).astype(jnp.float32)
    return jnp.stack([unit[0], local_block + unit[1], unit[2]]).astype(jnp.float32)


def draw_counts(key, part):
    first_key, second_key, third_key = jax.random.split(jax.random.fold_in(key, 11), 3)
    one_draw = jax.random.randint(first_key, (BLOCKS,), 1, CAP + 1)
    two_draw = jax.random.randint(second_key, (BLOCKS,), 1, CAP + 1)
    fuller = jax.random.randint(third_key, (), 0, BLOCKS)
    return jnp.where(jnp.arange(BLOCKS) == fuller, CAP, jnp.minimum(one_draw, two_draw)).astype(jnp.int32)


def draw_neighbours(key, part):
    width_all = 3 * BLK_DEV
    own_block = (jnp.arange(BLOCKS) % BLK_DEV)[:, None]
    candidate = jnp.arange(width_all)[None, :]
    nearby = jnp.abs(candidate % BLK_DEV - own_block) <= 1
    itself = (candidate // BLK_DEV == 1) & (candidate % BLK_DEV == own_block)
    scores = jax.random.randint(jax.random.fold_in(key, 23), (BLOCKS, width_all), 0, 65536) * 64 + candidate
    scores = jnp.where(nearby, scores, -1)
    scores = jnp.where(itself, 1 << 24, scores)
    ranked, chosen = lax.top_k(scores, NB)
    return chosen.astype(jnp.int32)


def draw_wavevectors(key, part):
    values = jax.random.randint(jax.random.fold_in(key, 37), (3, K), -4, 5)
    vacant = jnp.all(values == 0, axis=0)
    first_row = jnp.where(vacant, 1, values[0])
    return jnp.concatenate([first_row[None], values[1:]], 0).astype(jnp.int32)


def levels(own_key, shape, pieces, least, top_value):
    loudness, own = 1.0, jax.random.fold_in(own_key, 6)
    for axis_at, blocks in pieces:
        draws = jnp.exp(jax.random.uniform(jax.random.fold_in(own, axis_at), (blocks,), jnp.float32, least / len(pieces), top_value / len(pieces)))
        loudness = loudness * jnp.repeat(draws, shape[axis_at] // blocks).reshape([-1 if axis == axis_at else 1 for axis in range(len(shape))])
    return loudness


def gaussian(own_key, extent, spread, most, shards=(), kind=jnp.bfloat16):
    values = spread * jax.random.normal(own_key, extent, jnp.float32)
    if shards:
        values = values * levels(own_key, extent, shards, -0.22, 0.18)
    return jnp.clip(values, -most, most).astype(kind)


def setup_inputs(seed: int = 0) -> dict:
    arg_keys = jax.random.split(jax.random.key(seed), 8)
    return {
        "features": gaussian(arg_keys[0], (C, SLOTS), 1.0, 6.0, ((0, 4), (1, 64)), jnp.float32),
        "positions": draw_positions(jax.random.fold_in(arg_keys[7], 71), 0),
        "counts": draw_counts(jax.random.fold_in(arg_keys[7], 71), 0),
        "neighbours": draw_neighbours(jax.random.fold_in(arg_keys[7], 71), 0),
        "wavevectors": draw_wavevectors(jax.random.fold_in(arg_keys[7], 71), 0),
        "filters": gaussian(arg_keys[5], (NRAD, C, C), (NRAD * C) ** -0.5, 0.125, ((1, 4),), jnp.float32),
        "cotangent": gaussian(arg_keys[6], (C, SLOTS), 1.0, 6.0, ((0, 4), (1, 64)), jnp.float32),
    }


slab_width = 1.0
pair_scale = 0.3
screen_alpha = 2000.0
screen_kappa = 100.0
wave_most = 128
highest = lax.Precision.HIGHEST

def radial_terms(own_place, far_place, offset):
    delta_x = own_place[0][:, None] - (far_place[0][None, :] + offset * slab_width)
    delta_y = own_place[1][:, None] - far_place[1][None, :]
    delta_z = own_place[2][:, None] - far_place[2][None, :]
    square = delta_x * delta_x + delta_y * delta_y + delta_z * delta_z
    distance = jnp.sqrt(square)
    envelope = jnp.maximum(1.0 - square, 0.0) ** 2
    centres = jnp.arange(NRAD, dtype=jnp.float32) + 0.5
    scaled = distance[None] * NRAD - centres[:, None, None]
    return pair_scale * jnp.exp(-0.5 * scaled * scaled) * envelope[None]

def wave_table(wavevectors, x_length, y_length):
    lengths = jnp.array([x_length, y_length, 1.0], jnp.float32)
    scaled = 2.0 * math.pi * wavevectors.astype(jnp.float32) / lengths[:, None]
    square = lax.optimization_barrier(jnp.sum(scaled * scaled, 0))
    screened = jnp.exp(-square / screen_alpha) / (square + screen_kappa)
    return (scaled, screened / jnp.sqrt(jnp.sum(screened * screened)))

def phase_block(wave_part, coords):
    return wave_part[0][:, None] * coords[0][None, :] + wave_part[1][:, None] * coords[1][None, :] + wave_part[2][:, None] * coords[2][None, :]

def structure(fields, coords, scaled):
    wave_block = min(K, wave_most)
    real_list = []
    imag_list = []
    for first_wave in range(0, K, wave_block):
        phases = phase_block(scaled[:, first_wave:first_wave + wave_block], coords)
        real_list.append(jnp.einsum('ci,ki->ck', fields, jnp.cos(phases), precision=highest))
        imag_list.append(jnp.einsum('ci,ki->ck', fields, jnp.sin(phases), precision=highest))
    return (jnp.concatenate(real_list, 1), jnp.concatenate(imag_list, 1))

def project_back(real_part, imag_part, coords, scaled, weights, factor):
    wave_block = min(K, wave_most)
    result = jnp.zeros((real_part.shape[0], coords.shape[1]), jnp.float32)
    for first_wave in range(0, K, wave_block):
        phases = phase_block(scaled[:, first_wave:first_wave + wave_block], coords)
        chosen = weights[first_wave:first_wave + wave_block]
        result = result + jnp.einsum('ck,ki->ci', real_part[:, first_wave:first_wave + wave_block] * chosen[None], jnp.cos(phases), precision=highest)
        result = result + jnp.einsum('ck,ki->ci', imag_part[:, first_wave:first_wave + wave_block] * chosen[None], jnp.sin(phases), precision=highest)
    return factor * result

def reference(features, positions, counts, neighbours, wavevectors, filters, cotangent):
    slots_layer = BLK_DEV * CAP
    slot_index = jnp.arange(SLOTS, dtype=jnp.int32)
    live_mask = (slot_index % CAP < jnp.repeat(counts, CAP, total_repeat_length=SLOTS)).astype(jnp.float32)
    masked = features * live_mask[None]
    cot_masked = cotangent * live_mask[None]

    def source_of(block_number, chosen):
        own_layer = block_number // BLK_DEV
        section = chosen // BLK_DEV
        source_layer = (own_layer + section - 1 + N_SPACE) % N_SPACE
        first_slot = ((source_layer * BLK_DEV + chosen % BLK_DEV) * CAP).astype(jnp.int32)
        return (first_slot, (section - 1).astype(jnp.float32))

    def pair_forward(block_number):
        own_place = lax.dynamic_slice_in_dim(positions, (block_number * CAP).astype(jnp.int32), CAP, 1)
        running = jnp.zeros((NRAD, C, CAP), jnp.float32)
        for entry_index in range(NB):
            first_slot, offset = source_of(block_number, neighbours[block_number, entry_index])
            far_place = lax.dynamic_slice_in_dim(positions, first_slot, CAP, 1)
            values = lax.dynamic_slice_in_dim(masked, first_slot, CAP, 1)
            radial = radial_terms(own_place, far_place, offset)
            running = running + jnp.einsum('cj,rij->rci', values, radial, precision=highest)
        return jnp.einsum('rcd,rci->di', filters, running, precision=highest)
    pre_blocks = lax.map(pair_forward, jnp.arange(BLOCKS, dtype=jnp.int32))
    pre = jnp.transpose(pre_blocks, (1, 0, 2)).reshape(C, SLOTS)
    layer_of = (slot_index // slots_layer).astype(jnp.float32)
    coords = jnp.stack([positions[0] + layer_of * slab_width, positions[1], positions[2]])
    scaled, weights = wave_table(wavevectors, N_SPACE * slab_width, BLK_DEV * 1.0)
    factor = math.sqrt(3.0 / SLOTS)
    real_part, imag_part = structure(masked, coords, scaled)
    long_forward = project_back(real_part, imag_part, coords, scaled, weights, factor)
    sigma = jax.nn.sigmoid(pre)
    updated = live_mask[None] * (masked + pre * sigma + long_forward)
    upstream = cot_masked * sigma * (1.0 + pre * (1.0 - sigma))

    def pair_backward(gradient, block_number):
        own_place = lax.dynamic_slice_in_dim(positions, (block_number * CAP).astype(jnp.int32), CAP, 1)
        cot_block = lax.dynamic_slice_in_dim(upstream, (block_number * CAP).astype(jnp.int32), CAP, 1)
        pair_cot = jnp.einsum('rcd,di->rci', filters, cot_block, precision=highest)
        for entry_index in range(NB):
            first_slot, offset = source_of(block_number, neighbours[block_number, entry_index])
            far_place = lax.dynamic_slice_in_dim(positions, first_slot, CAP, 1)
            radial = radial_terms(own_place, far_place, offset)
            contribution = jnp.einsum('rci,rij->cj', pair_cot, radial, precision=highest)
            current = lax.dynamic_slice_in_dim(gradient, first_slot, CAP, 1)
            gradient = lax.dynamic_update_slice_in_dim(gradient, current + contribution, first_slot, 1)
        return (gradient, None)
    pair_grad, _ = lax.scan(pair_backward, jnp.zeros((C, SLOTS), jnp.float32), jnp.arange(BLOCKS, dtype=jnp.int32))
    real_cot, imag_cot = structure(cot_masked, coords, scaled)
    long_adjoint = project_back(real_cot, imag_cot, coords, scaled, weights, factor)
    grad_features = live_mask[None] * (cot_masked + pair_grad + long_adjoint)
    return (updated, grad_features)
```

```python
import functools
import math

import jax
import jax.numpy as jnp
import numpy as np
from jax import lax
from jax.experimental import pallas as pl
from jax.experimental.pallas import tpu as pltpu
from jax.sharding import PartitionSpec as P

NRAD = 8
NB = 4
CAP = 256
LAYER = 512
HALF = 384
ROWS = 64
PACK = 72
CHUNK = 32
VMEM_BYTES = 56 << 20


vmem = pl.BlockSpec(memory_space=pltpu.VMEM)
smem = pl.BlockSpec(memory_space=pltpu.SMEM)
f32, bf16 = jnp.float32, jnp.bfloat16
NT = (((1,), (1,)), ((), ()))
NN = (((1,), (0,)), ((), ()))


def half_space():
    m = np.arange(HALF)
    nz = (m + 4) % 9 - 4
    rest = (m - nz) // 9
    ny = (rest + 4) % 9 - 4
    nx = (rest - ny) // 9
    return nx, ny, nz


def dot(a, b, dims=NN):
    return lax.dot_general(a, b, dims, preferred_element_type=f32)


def split(value):
    high = value.astype(bf16)
    return high, (value - high.astype(f32)).astype(bf16)


def shape(*dims, dtype=f32):
    return jax.ShapeDtypeStruct(dims, dtype)


def call(kernel, out, n_smem, n_vmem, scratch=(), name=None):
    many = isinstance(out, tuple)
    return pl.pallas_call(
        kernel,
        out_shape=out,
        in_specs=[smem] * n_smem + [vmem] * n_vmem,
        out_specs=tuple([vmem] * len(out)) if many else vmem,
        scratch_shapes=list(scratch),
        compiler_params=pltpu.CompilerParams(vmem_limit_bytes=VMEM_BYTES),
        name=name,
    )


def live_row(counts):
    lane = lax.broadcasted_iota(jnp.int32, (1, LAYER), 1)
    bound = jnp.where(lane < CAP, counts[0], counts[1] + CAP)
    return (lane < bound).astype(f32)


def pack_kernel(counts, features, positions, cotangent, packed, cot_masked):
    live = live_row(counts)
    packed[0:ROWS, :] = features[...] * live
    packed[ROWS : ROWS + 3, :] = positions[...]
    packed[ROWS + 3 : PACK, :] = jnp.broadcast_to(live, (PACK - ROWS - 3, LAYER))
    cot_masked[...] = cotangent[...] * live


def filter_kernel(filters, forward, backward):
    for r in range(NRAD):
        scaled = filters[r] * (0.3 * math.exp(-0.5 * (r - 3.5) ** 2))
        high, low = split(scaled)
        rows = slice(r * ROWS, (r + 1) * ROWS)
        backward[rows, 0:256] = high
        backward[rows, 256:512] = high
        backward[rows, 512:768] = low
    full = jnp.concatenate(
        [filters[r] * (0.3 * math.exp(-0.5 * (r - 3.5) ** 2)) for r in range(NRAD)], 0
    )
    high, low = split(full.T)
    forward[:, 0:512] = high
    forward[:, 512:1024] = low
    forward[:, 1024:1536] = high


def trig(turns):
    x = (turns - jnp.round(turns)) * math.pi
    y = x * x
    s = x * (1 + y * (-1 / 6 + y * (1 / 120 + y * (-1 / 5040 + y * (1 / 362880 + y * (-1 / 39916800 + y * (1 / 6227020800)))))))
    c = 1 + y * (-1 / 2 + y * (1 / 24 + y * (-1 / 720 + y * (1 / 40320 + y * (-1 / 3628800 + y * (1 / 479001600))))))
    return 1 - 2 * s * s, 2 * s * c


def structure_kernel(packed, cot_masked, digits, keep, send, table_high, table_low, sums):
    space = lax.axis_index("space")
    core, x = space % 2, (space // 2) % 4
    row_x = (packed[ROWS : ROWS + 1, :] + space.astype(f32)) * (1 / 64)
    row_y = packed[ROWS + 1 : ROWS + 2, :] * 0.5
    row_z = packed[ROWS + 2 : ROWS + 3, :]

    def chunk(step, carry):
        first = pl.multiple_of(step * CHUNK, CHUNK)
        rows = pl.ds(first, CHUNK)
        later = pl.ds(first + HALF, CHUNK)
        turns = digits[rows, 0:1] * row_x + digits[rows, 1:2] * row_y + digits[rows, 2:3] * row_z
        cos, sin = trig(turns)
        high, low = split(cos)
        table_high[rows, :] = high
        table_low[rows, :] = low
        high, low = split(sin)
        table_high[later, :] = high
        table_low[later, :] = low
        return carry

    lax.fori_loop(0, HALF // CHUNK, chunk, 0)
    masked_high, masked_low = split(packed[0:ROWS, :])
    cot_high, cot_low = split(cot_masked[...])
    fields = jnp.concatenate([masked_high, cot_high, masked_low, cot_low], 0)
    both = dot(fields, table_high[...], NT) + dot(fields, table_low[...], NT)
    sums[...] = both[:128] + both[128:]
    for d in range(4):
        rows = slice(16 * d, 16 * d + 16)
        place = 16 * jnp.bitwise_xor(x, d)
        keep[rows, :] = sums[pl.ds(pl.multiple_of(core * ROWS + place, 16), 16), :]
        send[rows, :] = sums[pl.ds(pl.multiple_of((1 - core) * ROWS + place, 16), 16), :]


def radial_tiles(col, row, offset):
    dx = col[0] - row[0] + offset
    dy = col[1] - row[1]
    dz = col[2] - row[2]
    square = jnp.minimum(dx * dx + dy * dy + dz * dz, 1.0)
    inside = 1.0 - square
    v = 8.0 * jnp.sqrt(square) - 4.0
    up = jnp.exp(0.5 * v)
    down = jnp.exp(-0.5 * v)
    base = inside * inside * jnp.exp(-0.5 * (v * v))
    tiles = [None] * NRAD
    tiles[4], tiles[3] = base * up, base * down
    up, down = up * up, down * down
    for k in range(3):
        tiles[5 + k] = tiles[4 + k] * up
        tiles[2 - k] = tiles[3 - k] * down
    return tiles


def forward_kernel(neighbours, own, below, above, filters, keep, send, places, values, high, low, sums, share):
    mine = lax.axis_index("chan")
    for section, source in enumerate((below, own, above)):
        places[section * LAYER : (section + 1) * LAYER, :] = source[ROWS:PACK, :].T
        v_high, v_low = split(source[0:ROWS, :])
        for side in range(2):
            lanes = slice(side * CAP, (side + 1) * CAP)
            values[2 * section + side, 0:ROWS, :] = v_high[:, lanes]
            values[2 * section + side, ROWS:128, :] = v_low[:, lanes]
    for block in range(2):
        lanes = slice(block * CAP, (block + 1) * CAP)
        row = [own[ROWS + a : ROWS + a + 1, lanes] for a in range(3)]

        def chunk(step, carry):
            entry, part = step // 8, step % 8
            chosen = neighbours[block, entry]
            offset = (chosen // 2 - 1).astype(f32)
            source = pl.ds(pl.multiple_of(chosen * CAP + part * CHUNK, CHUNK), CHUNK)
            col = [places[source, a : a + 1] for a in range(3)]
            target = pl.ds(pl.multiple_of(step * CHUNK, CHUNK), CHUNK)
            for r, tile in enumerate(radial_tiles(col, row, offset)):
                first, second = split(tile)
                high[r, target, :] = first
                low[r, target, :] = second
            return carry

        lax.fori_loop(0, NB * 8, chunk, 0)
        stacked = jnp.concatenate([values[neighbours[block, e]] for e in range(NB)], 1)
        for r in range(NRAD):
            both = dot(stacked, high[r]) + dot(stacked, low[r])
            first, second = split(both[:ROWS] + both[ROWS:])
            rows = slice(r * ROWS, (r + 1) * ROWS)
            sums[rows, :] = first
            sums[512 + r * ROWS : 512 + (r + 1) * ROWS, :] = first
            sums[1024 + r * ROWS : 1024 + (r + 1) * ROWS, :] = second
        share[:, lanes] = dot(filters[...], sums[...])
    for k, flip in enumerate((0, 3, 1, 2)):
        panel = share[pl.ds(pl.multiple_of(ROWS * jnp.bitwise_xor(mine, flip), ROWS), ROWS), :]
        (keep if k < 2 else send)[(k % 2) * ROWS : (k % 2 + 1) * ROWS, :] = panel


def backward_kernel(neighbours, own, below, above, filters, mine_up, third_up, other_up,
                    left, middle, right, places, panels, cots, high, low, returns):
    mine = lax.axis_index("chan")
    ups = [mine_up[...], third_up[...], other_up[0:ROWS, :], other_up[ROWS:128, :]]
    for value, flip in zip(ups, (0, 3, 1, 2)):
        first, second = split(value)
        at = ROWS * jnp.bitwise_xor(mine, flip)
        panels[pl.ds(pl.multiple_of(at, ROWS), ROWS), :] = first
        panels[pl.ds(pl.multiple_of(at + 256, ROWS), ROWS), :] = second
        panels[pl.ds(pl.multiple_of(at + 512, ROWS), ROWS), :] = first
    places[...] = own[ROWS:PACK, :].T
    for r in range(NRAD):
        rows = slice(r * ROWS, (r + 1) * ROWS)
        first, second = split(dot(filters[rows, :], panels[...]))
        for block in range(2):
            lanes = slice(block * CAP, (block + 1) * CAP)
            cots[block, 0:ROWS, r * CAP : (r + 1) * CAP] = first[:, lanes]
            cots[block, ROWS:128, r * CAP : (r + 1) * CAP] = second[:, lanes]
    returns[...] = jnp.zeros_like(returns)
    for block in range(2):

        def entry_step(entry, carry):
            chosen = neighbours[block, entry]
            section = chosen // 2
            offset = (section - 1).astype(f32)
            side = pl.multiple_of((chosen % 2) * CAP, CAP)
            lanes = pl.ds(side, CAP)
            row = []
            for a in range(3):
                line = slice(ROWS + a, ROWS + a + 1)
                near = jnp.where(section == 0, below[line, lanes], above[line, lanes])
                row.append(jnp.where(section == 1, own[line, lanes], near))

            def chunk(part, inner):
                at = pl.multiple_of(part * CHUNK, CHUNK)
                source = pl.ds(pl.multiple_of(block * CAP + at, CHUNK), CHUNK)
                col = [places[source, a : a + 1] for a in range(3)]
                for r, tile in enumerate(radial_tiles(col, row, -offset)):
                    first, second = split(tile)
                    high[pl.ds(r * CAP + at, CHUNK), :] = first
                    low[pl.ds(r * CAP + at, CHUNK), :] = second
                return inner

            lax.fori_loop(0, 8, chunk, 0)
            both = dot(cots[block], high[...]) + dot(cots[block], low[...])
            returns[chosen] = returns[chosen] + both[:ROWS] + both[ROWS:]
            return carry

        lax.fori_loop(0, NB, entry_step, 0)
    for section, out in enumerate((left, middle, right)):
        out[:, 0:CAP] = returns[2 * section]
        out[:, CAP:LAYER] = returns[2 * section + 1]


def project_kernel(mine_half, other_half, weights, table_high, table_low, long, scratch):
    space = lax.axis_index("space")
    core, x = space % 2, (space // 2) % 4
    for half, at in ((mine_half, core), (other_half, 1 - core)):
        scaled = half[...] * weights[...]
        for d in range(4):
            place = at * ROWS + 16 * jnp.bitwise_xor(x, d)
            first, second = split(scaled[16 * d : 16 * d + 16])
            scratch[pl.ds(pl.multiple_of(place, 16), 16), :] = first
            scratch[pl.ds(pl.multiple_of(place + 128, 16), 16), :] = second
    both = dot(scratch[...], table_high[...]) + dot(scratch[...], table_low[...])
    long[...] = both[:128] + both[128:]


def wave_weights(wavevectors, n_space, slots):
    code = jnp.abs(81 * wavevectors[0] + 9 * wavevectors[1] + wavevectors[2])
    copies = jnp.sum((code[:, None] == jnp.arange(HALF)[None, :]).astype(f32), 0)
    nx, ny, nz = half_space()
    qx, qy, qz = 2 * math.pi / 64 * nx, math.pi * ny, 2 * math.pi * nz
    square = qx * qx + qy * qy + qz * qz
    screened = jnp.asarray(np.exp(-square / 2000.0) / (square + 100.0), f32)
    factor = math.sqrt(3.0 / (n_space * slots))
    weights = factor * copies * screened / jnp.sqrt(jnp.sum(copies * screened * screened))
    return jnp.concatenate([weights, weights])[None]


def shards(features, positions, counts, neighbours, wavevectors, filters, cotangent):
    n_space = lax.axis_size("space")

    def shift(v, d):
        return lax.ppermute(v, "space", [(i, (i + d) % n_space) for i in range(n_space)])

    def swap(v, mask):
        return lax.ppermute(v, "space", [(i, i ^ mask) for i in range(n_space)])

    def chan_swap(v, mask):
        return lax.ppermute(v, "chan", [(i, i ^ mask) for i in range(4)])

    packed, cot_masked = call(
        pack_kernel, (shape(PACK, LAYER), shape(ROWS, LAYER)), 1, 3, name="pack"
    )(counts, features, positions, cotangent)
    below = shift(packed, 1)
    above = shift(packed, -1)

    digits = np.zeros((HALF, 8), np.float32)
    digits[:, :3] = np.stack(half_space(), 1)
    keep, send, table_high, table_low = call(
        structure_kernel,
        (shape(ROWS, 768), shape(ROWS, 768), shape(768, LAYER, dtype=bf16), shape(768, LAYER, dtype=bf16)),
        0, 3, [pltpu.VMEM((128, 768), f32)], name="structure",
    )(packed, cot_masked, jnp.asarray(digits))
    forward_filters, backward_filters = call(
        filter_kernel, (shape(256, 1536, dtype=bf16), shape(512, 768, dtype=bf16)), 0, 1, name="filters"
    )(filters)
    weights = wave_weights(wavevectors, n_space, LAYER)

    half = keep + swap(send, 1)
    got = [swap(half[16 * d : 16 * d + 16], 2 * d) for d in (1, 2, 3)]
    quarter = half[:16] + got[0] + got[1] + got[2]
    for mask in (8, 16, 32):
        quarter = quarter + swap(quarter, mask)
    half = jnp.concatenate([quarter] + [swap(quarter, 2 * d) for d in (1, 2, 3)], 0)
    other = swap(half, 1)
    long = call(
        project_kernel, shape(128, LAYER), 0, 5, [pltpu.VMEM((256, 768), bf16)], name="project"
    )(half, other, weights, table_high, table_low)

    keep, send = call(
        forward_kernel, (shape(128, LAYER), shape(128, LAYER)), 1, 4,
        [
            pltpu.VMEM((3 * LAYER, 8), f32),
            pltpu.VMEM((6, 128, CAP), bf16),
            pltpu.VMEM((NRAD, NB * CAP, CAP), bf16),
            pltpu.VMEM((NRAD, NB * CAP, CAP), bf16),
            pltpu.VMEM((1536, CAP), bf16),
            pltpu.VMEM((256, LAYER), f32),
        ],
        name="forward",
    )(neighbours, packed, below, above, forward_filters)
    keep = keep + chan_swap(send, 1)
    pre = keep[:ROWS] + chan_swap(keep[ROWS:], 3)
    sigma = jax.nn.sigmoid(pre)
    activated = pre * sigma
    upstream = cot_masked * sigma * (1.0 + pre * (1.0 - sigma))
    third = chan_swap(upstream, 3)
    other_up = chan_swap(jnp.concatenate([upstream, third], 0), 1)
    left, middle, right = call(
        backward_kernel, tuple([shape(ROWS, LAYER)] * 3), 1, 7,
        [
            pltpu.VMEM((LAYER, 8), f32),
            pltpu.VMEM((768, LAYER), bf16),
            pltpu.VMEM((2, 128, NRAD * CAP), bf16),
            pltpu.VMEM((NRAD * CAP, CAP), bf16),
            pltpu.VMEM((NRAD * CAP, CAP), bf16),
            pltpu.VMEM((6, ROWS, CAP), f32),
        ],
        name="backward",
    )(neighbours, packed, below, above, backward_filters, upstream, third, other_up)
    from_lower = shift(right, 1)
    from_upper = shift(left, -1)
    live = packed[ROWS + 3][None]
    updated = live * (packed[:ROWS] + activated + long[:ROWS])
    grad_features = live * (cot_masked + middle + from_lower + from_upper + long[ROWS:])
    return updated, grad_features


def solution(mesh):
    return jax.shard_map(
        shards,
        mesh=mesh,
        in_specs=(
            P("chan", "space"),
            P(None, "space"),
            P("space"),
            P("space", None),
            P(),
            P(None, "chan", None),
            P("chan", "space"),
        ),
        out_specs=(P("chan", "space"), P("chan", "space")),
        check_vma=False,
    )
```

```python
import math

import jax
import jax.numpy as jnp
import numpy as np
from jax import lax
from jax.experimental import pallas as pl
from jax.experimental.pallas import tpu as pltpu
from jax.sharding import PartitionSpec as P

NRAD = 8
CAP = 256
LAYER = 512
HALF = 384
ROWS = 64
PACK = 72
CHUNK = 32
LOG2E = math.log2(math.e)
SCALE = 8.0 * LOG2E
TERM = [0.3 * math.exp(-0.5 * (r - 3.5) ** 2) / SCALE**4 for r in range(NRAD)]
VMEM_BYTES = 56 << 20


vmem = pl.BlockSpec(memory_space=pltpu.VMEM)
smem = pl.BlockSpec(memory_space=pltpu.SMEM)
f32, bf16 = jnp.float32, jnp.bfloat16
NT = (((1,), (1,)), ((), ()))
NN = (((1,), (0,)), ((), ()))


def half_space():
    m = np.arange(HALF)
    nz = (m + 4) % 9 - 4
    rest = (m - nz) // 9
    ny = (rest + 4) % 9 - 4
    nx = (rest - ny) // 9
    return nx, ny, nz


def dot(a, b, dims=NN):
    return lax.dot_general(a, b, dims, preferred_element_type=f32)


def split(value):
    high = value.astype(bf16)
    return high, (value - high.astype(f32)).astype(bf16)


def shape(*dims, dtype=f32):
    return jax.ShapeDtypeStruct(dims, dtype)


def call(kernel, out, n_smem, n_vmem, scratch=()):
    many = isinstance(out, tuple)
    return pl.pallas_call(
        kernel,
        out_shape=out,
        in_specs=[smem] * n_smem + [vmem] * n_vmem,
        out_specs=tuple([vmem] * len(out)) if many else vmem,
        scratch_shapes=list(scratch),
        compiler_params=pltpu.CompilerParams(vmem_limit_bytes=VMEM_BYTES),
    )


def live_row(counts):
    lane = lax.broadcasted_iota(jnp.int32, (1, LAYER), 1)
    bound = jnp.where(lane < CAP, counts[0], counts[1] + CAP)
    return (lane < bound).astype(f32)


def pack_kernel(counts, features, positions, packed):
    live = live_row(counts)
    packed[0:ROWS, :] = features[...] * live
    packed[ROWS : ROWS + 3, :] = positions[...]
    packed[ROWS + 3 : PACK, :] = jnp.broadcast_to(live, (PACK - ROWS - 3, LAYER))


def filter_kernel(filters, forward, backward):
    scaled = jnp.concatenate([filters[r] * TERM[r] for r in range(NRAD)], 0)
    high, low = split(scaled)
    backward[:, 0:256] = high
    backward[:, 256:512] = high
    backward[:, 512:768] = low
    high, low = split(scaled.T)
    forward[:, 0:512] = high
    forward[:, 512:1024] = low
    forward[:, 1024:1536] = high


def trig(turns):
    x = (turns - jnp.round(turns)) * math.pi
    y = x * x
    s = x * (1 + y * (-1 / 6 + y * (1 / 120 + y * (-1 / 5040 + y * (1 / 362880 + y * (-1 / 39916800 + y * (1 / 6227020800)))))))
    c = 1 + y * (-1 / 2 + y * (1 / 24 + y * (-1 / 720 + y * (1 / 40320 + y * (-1 / 3628800 + y * (1 / 479001600))))))
    return 1 - 2 * s * s, 2 * s * c


def structure_kernel(packed, cotangent, digits, keep, send, cot_masked, table_high, table_low, sums):
    space = lax.axis_index("space")
    core, x = space % 2, (space // 2) % 4
    row_x = (packed[ROWS : ROWS + 1, :] + space.astype(f32)) * (1 / 64)
    row_y = packed[ROWS + 1 : ROWS + 2, :] * 0.5
    row_z = packed[ROWS + 2 : ROWS + 3, :]

    def chunk(step, carry):
        first = pl.multiple_of(step * CHUNK, CHUNK)
        rows = pl.ds(first, CHUNK)
        later = pl.ds(first + HALF, CHUNK)
        turns = digits[rows, 0:1] * row_x + digits[rows, 1:2] * row_y + digits[rows, 2:3] * row_z
        cos, sin = trig(turns)
        high, low = split(cos)
        table_high[rows, :] = high
        table_low[rows, :] = low
        high, low = split(sin)
        table_high[later, :] = high
        table_low[later, :] = low
        return carry

    lax.fori_loop(0, HALF // CHUNK, chunk, 0)
    masked_high, masked_low = split(packed[0:ROWS, :])
    cot = cotangent[...] * packed[ROWS + 3 : ROWS + 4, :]
    cot_masked[...] = cot
    cot_high, cot_low = split(cot)
    fields = jnp.concatenate([masked_high, cot_high, masked_low, cot_low], 0)
    both = dot(fields, table_high[...], NT) + dot(fields, table_low[...], NT)
    sums[...] = both[:128] + both[128:]
    for d in range(4):
        rows = slice(16 * d, 16 * d + 16)
        place = 16 * jnp.bitwise_xor(x, d)
        keep[rows, :] = sums[pl.ds(pl.multiple_of(core * ROWS + place, 16), 16), :]
        send[rows, :] = sums[pl.ds(pl.multiple_of((1 - core) * ROWS + place, 16), 16), :]


def radial_terms(col, row):
    dx, dy, dz = (col[a] - row[a] for a in range(3))
    square = jnp.minimum(dx * dx + dy * dy + dz * dz, SCALE * SCALE)
    inside = SCALE * SCALE - square
    u = square * lax.rsqrt(jnp.maximum(square, 1e-20)) - 4.0 * LOG2E
    bend = u * (0.5 / LOG2E)
    base = inside * inside
    up, down = jnp.exp2(u), jnp.exp2(-u)
    terms = [None] * NRAD
    terms[4] = base * jnp.exp2(u * (0.5 - bend))
    terms[3] = base * jnp.exp2(u * (-0.5 - bend))
    for k in range(3):
        terms[5 + k] = terms[4 + k] * up
        terms[2 - k] = terms[3 - k] * down
    return terms


def layer_setup(sources, columns, lines, amounts):
    own = sources[1]
    flipped = own[ROWS:PACK, :].T * SCALE
    for a in range(3):
        columns[a] = jnp.broadcast_to(flipped[:, a : a + 1], (LAYER, 128))
    for section, source in enumerate(sources):
        for side in range(2):
            lanes = slice(side * CAP, (side + 1) * CAP)
            amounts[2 * section + side] = jnp.sum(source[ROWS + 3 : ROWS + 4, lanes]).astype(jnp.int32)
        for side in range(4):
            for a in range(3):
                at = slice(ROWS + a, ROWS + a + 1)
                shift = (section - 1.0) * SCALE if a == 0 else 0.0
                lines[4 * section + side, a : a + 1, :] = source[at, 128 * side : 128 * side + 128] * SCALE + shift


def visit(neighbours, amounts, columns, lines, flush, store):
    def outer(index, carry):
        block, entry, side = index // 8, (index // 2) % 4, index % 2
        chosen = neighbours[block, entry]
        piece = 2 * chosen + side
        trips = jnp.where(side * 128 < amounts[chosen], (amounts[2 + block] + 127) // 128, 0)

        def inner(step, last):
            flush(*last)
            where = 2 * block + step
            at = pl.ds(pl.multiple_of(where * 128, 128), 128)
            col = [columns[a, at, :] for a in range(3)]
            row = [lines[piece, a : a + 1, :] for a in range(3)]
            store(radial_terms(col, row))
            return where, piece

        return lax.fori_loop(0, trips, inner, carry)

    flush(*lax.fori_loop(0, 16, outer, (jnp.int32(0), jnp.int32(0))))


def forward_kernel(neighbours, own, below, above, filters, own_panel, third_panel, near_panel, far_panel,
                   columns, lines, amounts, values, highs, lows, sums, share):
    mine = lax.axis_index("chan")
    layer_setup((below, own, above), columns, lines, amounts)
    for section, source in enumerate((below, own, above)):
        high, low = split(source[0:ROWS, :])
        for side in range(4):
            values[4 * section + side, 0:ROWS, :] = high[:, 128 * side : 128 * side + 128]
            values[4 * section + side, ROWS:128, :] = low[:, 128 * side : 128 * side + 128]
    sums[...] = jnp.zeros_like(sums)
    highs[...] = jnp.zeros_like(highs)
    lows[...] = jnp.zeros_like(lows)

    def flush(where, piece):
        value = values[piece]
        out = dot(
            jnp.concatenate([highs[...], lows[...]], 1), jnp.concatenate([value, value], 1), NT
        )
        rows = pl.ds(pl.multiple_of(where * 1024, 1024), 1024)
        sums[rows, :] = sums[rows, :] + out

    def store(terms):
        for r, term in enumerate(terms):
            high, low = split(term)
            highs[128 * r : 128 * r + 128, :] = high
            lows[128 * r : 128 * r + 128, :] = low

    visit(neighbours, amounts, columns, lines, flush, store)
    lane = lax.broadcasted_iota(jnp.int32, (128, 128), 1)
    for where in range(4):
        pieces = []
        for r in range(0, NRAD, 2):
            even = sums[where * 1024 + 128 * r : where * 1024 + 128 * r + 128, :]
            odd = sums[where * 1024 + 128 * r + 128 : where * 1024 + 128 * r + 256, :]
            pieces.append(
                jnp.where(lane < ROWS, even, odd)
                + jnp.where(lane < ROWS, pltpu.roll(even, ROWS, 1), pltpu.roll(odd, ROWS, 1))
            )
        first, second = zip(*[split(p) for p in pieces])
        right = jnp.concatenate([*first, *first, *second], 1)
        share[:, 128 * where : 128 * where + 128] = dot(filters[...], right, NT)
    for out, flip in ((own_panel, 0), (third_panel, 3), (near_panel, 1), (far_panel, 2)):
        out[...] = share[pl.ds(pl.multiple_of(ROWS * jnp.bitwise_xor(mine, flip), ROWS), ROWS), :]


def activation_kernel(own_panel, near, third, cot_masked, activated, upstream):
    pre = own_panel[...] + near[...] + third[...]
    sigma = 1.0 / (1.0 + jnp.exp(-pre))
    activated[...] = pre * sigma
    upstream[...] = cot_masked[...] * (sigma * (1.0 + pre * (1.0 - sigma)))


def backward_kernel(neighbours, own, below, above, filters, mine_up, third_up, near_up, far_up,
                    left, middle, right, columns, lines, amounts, panels, cots, tiles, sums):
    mine = lax.axis_index("chan")
    layer_setup((below, own, above), columns, lines, amounts)
    ups = [mine_up[...], third_up[...], near_up[...], far_up[...]]
    for value, flip in zip(ups, (0, 3, 1, 2)):
        first, second = split(value)
        at = ROWS * jnp.bitwise_xor(mine, flip)
        panels[pl.ds(pl.multiple_of(at, ROWS), ROWS), :] = first
        panels[pl.ds(pl.multiple_of(at + 256, ROWS), ROWS), :] = second
        panels[pl.ds(pl.multiple_of(at + 512, ROWS), ROWS), :] = first
    cot = dot(filters[...], panels[...])
    for r in range(NRAD):
        first, second = split(cot[ROWS * r : ROWS * r + ROWS])
        for where in range(4):
            cots[NRAD * where + r, 0:ROWS, :] = first[:, 128 * where : 128 * where + 128]
            cots[NRAD * where + r, ROWS:128, :] = second[:, 128 * where : 128 * where + 128]
    sums[...] = jnp.zeros_like(sums)
    tiles[...] = jnp.zeros_like(tiles)

    def flush(where, piece):
        parts = []
        for r in range(NRAD):
            parts += [cots[NRAD * where + r]] * 2
        rows = pl.ds(pl.multiple_of(piece * 128, 128), 128)
        sums[rows, :] = sums[rows, :] + dot(jnp.concatenate(parts, 1), tiles[...])

    def store(terms):
        for r, term in enumerate(terms):
            high, low = split(term)
            tiles[256 * r : 256 * r + 128, :] = high
            tiles[256 * r + 128 : 256 * r + 256, :] = low

    visit(neighbours, amounts, columns, lines, flush, store)
    for section, out in enumerate((left, middle, right)):
        for side in range(4):
            at = 128 * (4 * section + side)
            out[:, 128 * side : 128 * side + 128] = sums[at : at + ROWS, :] + sums[at + ROWS : at + 128, :]


def project_kernel(mine_half, other_half, weights, table_high, table_low, packed, activated, cot_masked, middle,
                   updated, partial, scratch):
    space = lax.axis_index("space")
    core, x = space % 2, (space // 2) % 4
    for half, at in ((mine_half, core), (other_half, 1 - core)):
        scaled = half[...] * weights[...]
        for d in range(4):
            place = at * ROWS + 16 * jnp.bitwise_xor(x, d)
            first, second = split(scaled[16 * d : 16 * d + 16])
            scratch[pl.ds(pl.multiple_of(place, 16), 16), :] = first
            scratch[pl.ds(pl.multiple_of(place + 128, 16), 16), :] = second
    both = dot(scratch[...], table_high[...]) + dot(scratch[...], table_low[...])
    live = packed[ROWS + 3 : ROWS + 4, :]
    updated[...] = live * (packed[0:ROWS, :] + activated[...] + (both[:ROWS] + both[128 : 128 + ROWS]))
    partial[...] = live * (cot_masked[...] + middle[...] + (both[ROWS:128] + both[128 + ROWS :]))


def wave_weights(wavevectors, n_space, slots):
    code = jnp.abs(81 * wavevectors[0] + 9 * wavevectors[1] + wavevectors[2])
    copies = jnp.sum((code[:, None] == jnp.arange(HALF)[None, :]).astype(f32), 0)
    nx, ny, nz = half_space()
    qx, qy, qz = 2 * math.pi / 64 * nx, math.pi * ny, 2 * math.pi * nz
    square = qx * qx + qy * qy + qz * qz
    screened = jnp.asarray(np.exp(-square / 2000.0) / (square + 100.0), f32)
    factor = math.sqrt(3.0 / (n_space * slots))
    weights = factor * copies * screened / jnp.sqrt(jnp.sum(copies * screened * screened))
    return jnp.concatenate([weights, weights])[None]


def shards(features, positions, counts, neighbours, wavevectors, filters, cotangent):
    n_space = lax.axis_size("space")

    def shift(v, d):
        return lax.ppermute(v, "space", [(i, (i + d) % n_space) for i in range(n_space)])

    def swap(v, mask):
        return lax.ppermute(v, "space", [(i, i ^ mask) for i in range(n_space)])

    def chan_swap(v, mask):
        return lax.ppermute(v, "chan", [(i, i ^ mask) for i in range(4)])

    packed = call(pack_kernel, shape(PACK, LAYER), 1, 2)(counts, features, positions)
    below = shift(packed, 1)
    above = shift(packed, -1)

    digits = np.zeros((HALF, 8), np.float32)
    digits[:, :3] = np.stack(half_space(), 1)
    keep, send, cot_masked, table_high, table_low = call(
        structure_kernel,
        (shape(ROWS, 768), shape(ROWS, 768), shape(ROWS, LAYER),
         shape(768, LAYER, dtype=bf16), shape(768, LAYER, dtype=bf16)),
        0, 3, [pltpu.VMEM((128, 768), f32)],
    )(packed, cotangent, jnp.asarray(digits))
    forward_filters, backward_filters = call(
        filter_kernel, (shape(256, 1536, dtype=bf16), shape(512, 768, dtype=bf16)), 0, 1
    )(filters)
    weights = wave_weights(wavevectors, n_space, LAYER)

    half = keep + swap(send, 1)
    got = []
    for d in (1, 2, 3):
        got.append(swap(half[16 * d : 16 * d + 16], 2 * d))

    own_panel, third_panel, near_panel, far_panel = call(
        forward_kernel, tuple([shape(ROWS, LAYER)] * 4), 1, 4,
        [
            pltpu.VMEM((3, LAYER, 128), f32),
            pltpu.VMEM((12, 8, 128), f32),
            pltpu.SMEM((6,), jnp.int32),
            pltpu.VMEM((12, 128, 128), bf16),
            pltpu.VMEM((1024, 128), bf16),
            pltpu.VMEM((1024, 128), bf16),
            pltpu.VMEM((4096, 128), f32),
            pltpu.VMEM((256, LAYER), f32),
        ],
    )(neighbours, packed, below, above, forward_filters)
    quarter = half[:16] + got[0] + got[1] + got[2]
    far = chan_swap(far_panel, 1)
    near = chan_swap(near_panel, 1)
    quarter = quarter + swap(quarter, 32)
    third_panel = third_panel + far
    third = chan_swap(third_panel, 3)
    quarter = quarter + swap(quarter, 16)
    activated, upstream = call(
        activation_kernel, (shape(ROWS, LAYER), shape(ROWS, LAYER)), 0, 4
    )(own_panel, near, third, cot_masked)
    third_up = chan_swap(upstream, 3)
    near_up = chan_swap(upstream, 1)
    quarter = quarter + swap(quarter, 8)
    far_up = chan_swap(third_up, 1)
    got = []
    for d in (1, 2, 3):
        got.append(swap(quarter, 2 * d))
    left, middle, right = call(
        backward_kernel, tuple([shape(ROWS, LAYER)] * 3), 1, 8,
        [
            pltpu.VMEM((3, LAYER, 128), f32),
            pltpu.VMEM((12, 8, 128), f32),
            pltpu.SMEM((6,), jnp.int32),
            pltpu.VMEM((768, LAYER), bf16),
            pltpu.VMEM((32, 128, 128), bf16),
            pltpu.VMEM((2048, 128), bf16),
            pltpu.VMEM((1536, 128), f32),
        ],
    )(neighbours, packed, below, above, backward_filters, upstream, third_up, near_up, far_up)
    half = jnp.concatenate([quarter, *got], 0)
    from_lower = shift(right, 1)
    from_upper = shift(left, -1)
    other = swap(half, 1)
    updated, partial = call(
        project_kernel, (shape(ROWS, LAYER), shape(ROWS, LAYER)), 0, 9,
        [pltpu.VMEM((256, 768), bf16)],
    )(half, other, weights, table_high, table_low, packed, activated, cot_masked, middle)
    grad_features = partial + packed[ROWS + 3][None] * (from_lower + from_upper)
    return updated, grad_features


def solution(mesh):
    return jax.shard_map(
        shards,
        mesh=mesh,
        in_specs=(
            P("chan", "space"),
            P(None, "space"),
            P("space"),
            P("space", None),
            P(),
            P(None, "chan", None),
            P("chan", "space"),
        ),
        out_specs=(P("chan", "space"), P("chan", "space")),
        check_vma=False,
    )
```

```python
import math

import jax
import jax.numpy as jnp
import numpy as np
from jax import lax
from jax.experimental import pallas as pl
from jax.experimental.pallas import tpu as pltpu
from jax.sharding import PartitionSpec as P

NRAD = 8
CAP = 256
LAYER = 512
HALF = 384
ROWS = 64
PACK = 72
FACTOR = math.sqrt(3.0 / 32768.0)
LOG2E = math.log2(math.e)
SCALE = 8.0 * LOG2E
TERM = [0.3 * math.exp(-0.5 * (r - 3.5) ** 2) / SCALE**4 for r in range(NRAD)]
VMEM_BYTES = 24 << 20


vmem = pl.BlockSpec(memory_space=pltpu.VMEM)
smem = pl.BlockSpec(memory_space=pltpu.SMEM)
f32, bf16 = jnp.float32, jnp.bfloat16
NT = (((1,), (1,)), ((), ()))
NN = (((1,), (0,)), ((), ()))


def half_space():
    m = np.arange(HALF)
    plane = np.where(m < 360, m % 40 + 1, 0)
    ny = (plane + 4) % 9 - 4
    nx = (plane - ny) // 9
    nz = np.where(m < 360, m // 40 - 4, m - 359)
    return nx, ny, nz


def dot(a, b, dims=NN):
    return lax.dot_general(a, b, dims, preferred_element_type=f32)


def split(value):
    high = value.astype(bf16)
    return high, (value - high.astype(f32)).astype(bf16)


def shape(*dims, dtype=f32):
    return pltpu.VMEM(dims, dtype)


def call(kernel, out, n_smem, n_vmem, scratch=(), far=()):
    many = isinstance(out, tuple)
    run = pl.pallas_call(
        kernel,
        out_shape=out,
        in_specs=[smem] * n_smem + [vmem] * n_vmem,
        out_specs=tuple([vmem] * len(out)) if many else vmem,
        scratch_shapes=list(scratch),
        compiler_params=pltpu.CompilerParams(vmem_limit_bytes=VMEM_BYTES),
    )

    def place(*operands):
        put = pltpu.with_memory_space_constraint
        return run(
            *[put(v, pltpu.HBM if k < n_smem or k in far else pltpu.VMEM) for k, v in enumerate(operands)]
        )

    return place


def live_row(counts):
    lane = lax.broadcasted_iota(jnp.int32, (1, LAYER), 1)
    bound = jnp.where(lane < CAP, counts[0], counts[1] + CAP)
    return (lane < bound).astype(f32)


def pack_kernel(counts, features, positions, packed):
    live = live_row(counts)
    packed[0:ROWS, :] = features[...] * live
    packed[ROWS : ROWS + 3, :] = positions[...]
    packed[ROWS + 3 : PACK, :] = jnp.broadcast_to(live, (PACK - ROWS - 3, LAYER))


def forward_filter_kernel(filters, forward):
    for r in range(0, NRAD, 2):
        pair = jnp.concatenate([filters[r] * TERM[r], filters[r + 1] * TERM[r + 1]], 0)
        high, low = split(pair.T)
        for k in range(2):
            lanes = slice(ROWS * k, ROWS * k + ROWS)
            both_high = jnp.concatenate([high[:, lanes]] * 2, 1)
            both_low = jnp.concatenate([low[:, lanes]] * 2, 1)
            at = 128 * (r + k)
            forward[:, at : at + 128] = both_high
            forward[:, 1024 + at : 1024 + at + 128] = both_low
            forward[:, 2048 + at : 2048 + at + 128] = both_high


def backward_filter_kernel(filters, wavevectors, screened, backward, weights):
    for r in range(NRAD):
        rows = slice(ROWS * r, ROWS * r + ROWS)
        high, low = split(filters[r] * TERM[r])
        backward[rows, 0:256] = high
        backward[rows, 256:512] = high
        backward[rows, 512:768] = low
    plane, nz = 9 * wavevectors[0:1, :] + wavevectors[1:2, :], wavevectors[2:3, :]
    nz = jnp.where(plane < 0, -nz, nz)
    plane = jnp.abs(plane)
    code = jnp.where(plane > 0, 40 * (nz + 4) + plane - 1, 359 + jnp.abs(nz)).astype(f32)
    column = jnp.broadcast_to(code, (8, LAYER)).T[:, 0:1]
    lane = lax.broadcasted_iota(jnp.int32, (1, HALF), 1).astype(f32)
    copies = jnp.zeros((8, HALF), f32)
    for first in range(0, LAYER, 64):
        hit = jnp.where(column[first : first + 64] == lane, 1.0, 0.0)
        for k in range(0, 64, 8):
            copies = copies + hit[k : k + 8]
    copies = jnp.sum(copies, 0, keepdims=True)
    value = copies * screened[0:1, :]
    norm = jnp.sum(value * screened[0:1, :], 1, keepdims=True)
    value = value * (FACTOR / jnp.sqrt(norm))
    weights[...] = jnp.concatenate([value, value], 1)


def trig(turns):
    x = (turns - jnp.round(turns)) * math.pi
    y = x * x
    s = x * (1 + y * (-1 / 6 + y * (1 / 120 + y * (-1 / 5040 + y * (1 / 362880 + y * (-1 / 39916800 + y * (1 / 6227020800)))))))
    c = 1 + y * (-1 / 2 + y * (1 / 24 + y * (-1 / 720 + y * (1 / 40320 + y * (-1 / 3628800 + y * (1 / 479001600))))))
    return 1 - 2 * s * s, 2 * s * c


def structure_kernel(packed, cotangent, digits, keep, send, cot_masked, table_high, table_low, sums):
    space = lax.axis_index("space")
    core, x = space % 2, (space // 2) % 4
    row_x = (packed[ROWS : ROWS + 1, :] + space.astype(f32)) * (1 / 64)
    row_y = packed[ROWS + 1 : ROWS + 2, :] * 0.5
    row_z = packed[ROWS + 2 : ROWS + 3, :]

    def put(at, cos, sin):
        for base, value in ((at, cos), (HALF + at, sin)):
            high, low = split(value)
            table_high[base : base + value.shape[0], :] = high
            table_low[base : base + value.shape[0], :] = low

    tall = lax.broadcasted_iota(jnp.int32, (24, 1), 0).astype(f32) + 1.0
    cos_z, sin_z = trig(tall * row_z)
    put(360, cos_z, sin_z)
    cos_p, sin_p = trig(digits[0:40, 0:1] * row_x + digits[0:40, 1:2] * row_y)
    put(160, cos_p, sin_p)
    for n in range(1, 5):
        c, s = cos_z[n - 1 : n, :], sin_z[n - 1 : n, :]
        cc, ss, sc, cs = cos_p * c, sin_p * s, sin_p * c, cos_p * s
        put(160 + 40 * n, cc - ss, sc + cs)
        put(160 - 40 * n, cc + ss, sc - cs)
    masked_high, masked_low = split(packed[0:ROWS, :])
    cot = cotangent[...] * packed[ROWS + 3 : ROWS + 4, :]
    cot_masked[...] = cot
    cot_high, cot_low = split(cot)
    fields = jnp.concatenate([masked_high, cot_high, masked_low, cot_low], 0)
    both = dot(fields, table_high[...], NT) + dot(fields, table_low[...], NT)
    sums[...] = both[:128] + both[128:]
    for d in range(4):
        rows = slice(16 * d, 16 * d + 16)
        place = 16 * jnp.bitwise_xor(x, d)
        keep[rows, :] = sums[pl.ds(pl.multiple_of(core * ROWS + place, 16), 16), :]
        send[rows, :] = sums[pl.ds(pl.multiple_of((1 - core) * ROWS + place, 16), 16), :]


def radial_terms(col, row):
    dx, dy, dz = (col[a] - row[a] for a in range(3))
    square = jnp.minimum(dx * dx + dy * dy + dz * dz, SCALE * SCALE)
    inside = SCALE * SCALE - square
    u = square * lax.rsqrt(jnp.maximum(square, 1e-20)) - 4.0 * LOG2E
    bend = u * (0.5 / LOG2E)
    base = inside * inside
    up, down = jnp.exp2(u), jnp.exp2(-u)
    terms = [None] * NRAD
    terms[4] = base * jnp.exp2(u * (0.5 - bend))
    terms[3] = base * jnp.exp2(u * (-0.5 - bend))
    for k in range(3):
        terms[5 + k] = terms[4 + k] * up
        terms[2 - k] = terms[3 - k] * down
    return terms


def layer_setup(sources, columns, lines, amounts):
    own = sources[1]
    flipped = own[ROWS:PACK, :].T * SCALE
    for a in range(3):
        columns[a] = jnp.broadcast_to(flipped[:, a : a + 1], (LAYER, 128))
    for section, source in enumerate(sources):
        for side in range(2):
            lanes = slice(side * CAP, (side + 1) * CAP)
            amounts[2 * section + side] = jnp.sum(source[ROWS + 3 : ROWS + 4, lanes]).astype(jnp.int32)
        for side in range(4):
            for a in range(3):
                at = slice(ROWS + a, ROWS + a + 1)
                shift = (section - 1.0) * SCALE if a == 0 else 0.0
                lines[4 * section + side, a : a + 1, :] = source[at, 128 * side : 128 * side + 128] * SCALE + shift


def visit(neighbours, amounts, columns, lines, flush, store):
    def outer(index, carry):
        block, entry, side = index // 8, (index // 2) % 4, index % 2
        chosen = neighbours[block, entry]
        piece = 2 * chosen + side
        trips = jnp.where(side * 128 < amounts[chosen], (amounts[2 + block] + 127) // 128, 0)

        def inner(step, last):
            flush(*last)
            where = 2 * block + step
            at = pl.ds(pl.multiple_of(where * 128, 128), 128)
            col = [columns[a, at, :] for a in range(3)]
            row = [lines[piece, a : a + 1, :] for a in range(3)]
            store(radial_terms(col, row))
            return where, piece

        return lax.fori_loop(0, trips, inner, carry)

    flush(*lax.fori_loop(0, 16, outer, (jnp.int32(0), jnp.int32(0))))


def forward_kernel(neighbours, own, below, above, filters, own_panel, third_panel, near_panel, far_panel,
                   columns, lines, amounts, values, highs, lows, sums, share):
    mine = lax.axis_index("chan")
    layer_setup((below, own, above), columns, lines, amounts)
    for section, source in enumerate((below, own, above)):
        high, low = split(source[0:ROWS, :])
        for side in range(4):
            values[4 * section + side, 0:ROWS, :] = high[:, 128 * side : 128 * side + 128]
            values[4 * section + side, ROWS:128, :] = low[:, 128 * side : 128 * side + 128]
    sums[...] = jnp.zeros_like(sums)
    highs[...] = jnp.zeros_like(highs)
    lows[...] = jnp.zeros_like(lows)

    def flush(where, piece):
        value = values[piece]
        out = dot(
            jnp.concatenate([highs[...], lows[...]], 1), jnp.concatenate([value, value], 1), NT
        )
        rows = pl.ds(pl.multiple_of(where * 1024, 1024), 1024)
        sums[rows, :] = sums[rows, :] + out

    def store(terms):
        for r, term in enumerate(terms):
            high, low = split(term)
            highs[128 * r : 128 * r + 128, :] = high
            lows[128 * r : 128 * r + 128, :] = low

    visit(neighbours, amounts, columns, lines, flush, store)
    for pair in range(2):
        wheres = (2 * pair, 2 * pair + 1)
        first, second = [], []
        for r in range(NRAD):
            piece = jnp.concatenate(
                [sums[1024 * w + 128 * r : 1024 * w + 128 * r + 128, :] for w in wheres], 0
            )
            high, low = split(piece)
            first.append(high)
            second.append(low)
        share[:, 256 * pair : 256 * pair + 256] = dot(
            filters[...], jnp.concatenate([*first, *first, *second], 1), NT
        )
    for out, flip in ((own_panel, 0), (third_panel, 3), (near_panel, 1), (far_panel, 2)):
        out[...] = share[pl.ds(pl.multiple_of(ROWS * jnp.bitwise_xor(mine, flip), ROWS), ROWS), :]


def activation_kernel(own_panel, near, third, cot_masked, activated, upstream):
    pre = own_panel[...] + near[...] + third[...]
    sigma = 1.0 / (1.0 + jnp.exp(-pre))
    activated[...] = pre * sigma
    upstream[...] = cot_masked[...] * (sigma * (1.0 + pre * (1.0 - sigma)))


def backward_kernel(neighbours, own, below, above, filters, mine_up, third_up, near_up, far_up,
                    left, middle, right, columns, lines, amounts, panels, cots, tiles, sums):
    mine = lax.axis_index("chan")
    layer_setup((below, own, above), columns, lines, amounts)
    ups = [mine_up[...], third_up[...], near_up[...], far_up[...]]
    for value, flip in zip(ups, (0, 3, 1, 2)):
        first, second = split(value)
        at = ROWS * jnp.bitwise_xor(mine, flip)
        panels[pl.ds(pl.multiple_of(at, ROWS), ROWS), :] = first
        panels[pl.ds(pl.multiple_of(at + 256, ROWS), ROWS), :] = second
        panels[pl.ds(pl.multiple_of(at + 512, ROWS), ROWS), :] = first
    cot = dot(filters[...], panels[...])
    for r in range(NRAD):
        first, second = split(cot[ROWS * r : ROWS * r + ROWS])
        for where in range(4):
            cots[NRAD * where + r, 0:ROWS, :] = first[:, 128 * where : 128 * where + 128]
            cots[NRAD * where + r, ROWS:128, :] = second[:, 128 * where : 128 * where + 128]
    sums[...] = jnp.zeros_like(sums)
    tiles[...] = jnp.zeros_like(tiles)

    def flush(where, piece):
        parts = []
        for r in range(NRAD):
            parts += [cots[NRAD * where + r]] * 2
        rows = pl.ds(pl.multiple_of(piece * 128, 128), 128)
        sums[rows, :] = sums[rows, :] + dot(jnp.concatenate(parts, 1), tiles[...])

    def store(terms):
        for r, term in enumerate(terms):
            high, low = split(term)
            tiles[256 * r : 256 * r + 128, :] = high
            tiles[256 * r + 128 : 256 * r + 256, :] = low

    visit(neighbours, amounts, columns, lines, flush, store)
    for section, out in enumerate((left, middle, right)):
        for side in range(4):
            at = 128 * (4 * section + side)
            out[:, 128 * side : 128 * side + 128] = sums[at : at + ROWS, :] + sums[at + ROWS : at + 128, :]


def project_kernel(mine, one, two, three, weights, table_high, table_low, packed, activated, cot_masked, middle,
                   updated, partial, scratch):
    space = lax.axis_index("space")
    core, x = space % 2, (space // 2) % 4
    for d, piece in enumerate((mine, one, two, three)):
        first, second = split(piece[...] * weights[...])
        for half, at in ((0, core), (1, 1 - core)):
            rows = slice(16 * half, 16 * half + 16)
            place = at * ROWS + 16 * jnp.bitwise_xor(x, d)
            scratch[pl.ds(pl.multiple_of(place, 16), 16), :] = first[rows]
            scratch[pl.ds(pl.multiple_of(place + 128, 16), 16), :] = second[rows]
    both = dot(scratch[...], table_high[...]) + dot(scratch[...], table_low[...])
    live = packed[ROWS + 3 : ROWS + 4, :]
    updated[...] = live * (packed[0:ROWS, :] + activated[...] + (both[:ROWS] + both[128 : 128 + ROWS]))
    partial[...] = live * (cot_masked[...] + middle[...] + (both[ROWS:128] + both[128 + ROWS :]))


def screening():
    nx, ny, nz = half_space()
    qx, qy, qz = 2 * math.pi / 64 * nx, math.pi * ny, 2 * math.pi * nz
    square = qx * qx + qy * qy + qz * qz
    return np.tile((np.exp(-square / 2000.0) / (square + 100.0)).astype(np.float32), (8, 1))


def shards(features, positions, counts, neighbours, wavevectors, filters, cotangent):
    n_space = lax.axis_size("space")

    def shift(v, d):
        return lax.ppermute(v, "space", [(i, (i + d) % n_space) for i in range(n_space)])

    def swap(v, mask):
        return lax.ppermute(v, "space", [(i, i ^ mask) for i in range(n_space)])

    def chan_swap(v, mask):
        return lax.ppermute(v, "chan", [(i, i ^ mask) for i in range(4)])

    packed = call(pack_kernel, shape(PACK, LAYER), 1, 2, far=(1, 2))(counts, features, positions)
    below = shift(packed, 1)
    above = shift(packed, -1)

    digits = np.zeros((HALF, 8), np.float32)
    digits[:, :3] = np.stack(half_space(), 1)
    keep, send, cot_masked, table_high, table_low = call(
        structure_kernel,
        (shape(ROWS, 768), shape(ROWS, 768), shape(ROWS, LAYER),
         shape(768, LAYER, dtype=bf16), shape(768, LAYER, dtype=bf16)),
        0, 3, [pltpu.VMEM((128, 768), f32)], far=(1, 2),
    )(packed, cotangent, jnp.asarray(digits))
    forward_filters = call(forward_filter_kernel, shape(256, 3072, dtype=bf16), 0, 1, far=(0,))(filters)
    half = keep + swap(send, 1)
    got = []
    for d in (1, 2, 3):
        got.append(swap(half[16 * d : 16 * d + 16], 2 * d))

    own_panel, third_panel, near_panel, far_panel = call(
        forward_kernel, tuple([shape(ROWS, LAYER)] * 4), 1, 4,
        [
            pltpu.VMEM((3, LAYER, 128), f32),
            pltpu.VMEM((12, 8, 128), f32),
            pltpu.SMEM((6,), jnp.int32),
            pltpu.VMEM((12, 128, 128), bf16),
            pltpu.VMEM((1024, 128), bf16),
            pltpu.VMEM((1024, 128), bf16),
            pltpu.VMEM((4096, 128), f32),
            pltpu.VMEM((256, LAYER), f32),
        ],
    )(neighbours, packed, below, above, forward_filters)
    quarter = half[:16] + got[0] + got[1] + got[2]
    far = chan_swap(far_panel, 1)
    near = chan_swap(near_panel, 1)
    quarter = quarter + swap(quarter, 8)
    third_panel = third_panel + far
    third = chan_swap(third_panel, 3)
    quarter = quarter + swap(quarter, 32)
    backward_filters, weights = call(
        backward_filter_kernel, (shape(512, 768, dtype=bf16), shape(1, 768)), 0, 3,
        far=(0, 1, 2),
    )(filters, wavevectors, jnp.asarray(screening()))
    activated, upstream = call(
        activation_kernel, (shape(ROWS, LAYER), shape(ROWS, LAYER)), 0, 4
    )(own_panel, near, third, cot_masked)
    third_up = chan_swap(upstream, 3)
    near_up = chan_swap(upstream, 1)
    quarter = quarter + swap(quarter, 16)
    far_up = chan_swap(third_up, 1)
    pair = jnp.concatenate([quarter, swap(quarter, 1)], 0)
    got = []
    for d in (1, 2, 3):
        got.append(swap(pair, 2 * d))
    left, middle, right = call(
        backward_kernel, tuple([shape(ROWS, LAYER)] * 3), 1, 8,
        [
            pltpu.VMEM((3, LAYER, 128), f32),
            pltpu.VMEM((12, 8, 128), f32),
            pltpu.SMEM((6,), jnp.int32),
            pltpu.VMEM((768, LAYER), bf16),
            pltpu.VMEM((32, 128, 128), bf16),
            pltpu.VMEM((2048, 128), bf16),
            pltpu.VMEM((1536, 128), f32),
        ],
    )(neighbours, packed, below, above, backward_filters, upstream, third_up, near_up, far_up)
    from_lower = shift(right, 1)
    from_upper = shift(left, -1)
    updated, partial = call(
        project_kernel, (jax.ShapeDtypeStruct((ROWS, LAYER), f32), shape(ROWS, LAYER)), 0, 11,
        [pltpu.VMEM((256, 768), bf16)],
    )(pair, *got, weights, table_high, table_low, packed, activated, cot_masked, middle)
    grad_features = partial + packed[ROWS + 3][None] * (from_lower + from_upper)
    return updated, grad_features


def solution(mesh):
    return jax.shard_map(
        shards,
        mesh=mesh,
        in_specs=(
            P("chan", "space"),
            P(None, "space"),
            P("space"),
            P("space", None),
            P(),
            P(None, "chan", None),
            P("chan", "space"),
        ),
        out_specs=(P("chan", "space"), P("chan", "space")),
        check_vma=False,
    )
```

```python
import math

import jax
import jax.numpy as jnp
import numpy as np
from jax import lax
from jax.experimental import pallas as pl
from jax.experimental.pallas import tpu as pltpu
from jax.sharding import PartitionSpec as P

NRAD = 8
NB = 4
CAP = 256
LAYER = 512
HALF = 384
ROWS = 64
PACK = 72
FACTOR = math.sqrt(3.0 / 32768.0)
LOG2E = math.log2(math.e)
SCALE = 8.0 * LOG2E
TERM = [0.3 * math.exp(-0.5 * (r - 3.5) ** 2) / SCALE**4 for r in range(NRAD)]
VMEM_BYTES = 24 << 20


vmem = pl.BlockSpec(memory_space=pltpu.VMEM)
smem = pl.BlockSpec(memory_space=pltpu.SMEM)
f32, bf16 = jnp.float32, jnp.bfloat16
NT = (((1,), (1,)), ((), ()))
NN = (((1,), (0,)), ((), ()))


def half_space():
    m = np.arange(HALF)
    plane = np.where(m < 360, m % 40 + 1, 0)
    ny = (plane + 4) % 9 - 4
    nx = (plane - ny) // 9
    nz = np.where(m < 360, m // 40 - 4, m - 359)
    return nx, ny, nz


def dot(a, b, dims=NN):
    return lax.dot_general(a, b, dims, preferred_element_type=f32)


def split(value):
    high = value.astype(bf16)
    return high, (value - high.astype(f32)).astype(bf16)


def shape(*dims, dtype=f32):
    return pltpu.VMEM(dims, dtype)


def call(kernel, out, n_smem, n_vmem, scratch=(), far=()):
    many = isinstance(out, tuple)
    run = pl.pallas_call(
        kernel,
        out_shape=out,
        in_specs=[smem] * n_smem + [vmem] * n_vmem,
        out_specs=tuple([vmem] * len(out)) if many else vmem,
        scratch_shapes=list(scratch),
        compiler_params=pltpu.CompilerParams(vmem_limit_bytes=VMEM_BYTES),
    )

    def place(*operands):
        put = pltpu.with_memory_space_constraint
        return run(
            *[put(v, pltpu.HBM if k < n_smem or k in far else pltpu.VMEM) for k, v in enumerate(operands)]
        )

    return place


def live_row(counts):
    lane = lax.broadcasted_iota(jnp.int32, (1, LAYER), 1)
    bound = jnp.where(lane < CAP, counts[0], counts[1] + CAP)
    return (lane < bound).astype(f32)


def pack_kernel(counts, features, positions, packed):
    live = live_row(counts)
    packed[0:ROWS, :] = features[...] * live
    packed[ROWS : ROWS + 3, :] = positions[...]
    packed[ROWS + 3 : PACK, :] = jnp.broadcast_to(live, (PACK - ROWS - 3, LAYER))


def forward_filter_kernel(filters, forward):
    scaled = jnp.concatenate([filters[r] * TERM[r] for r in range(NRAD)], 0)
    high, low = split(scaled.T)
    forward[:, 0:512] = high
    forward[:, 512:1024] = low
    forward[:, 1024:1536] = high


def backward_filter_kernel(filters, wavevectors, screened, backward, weights):
    for r in range(NRAD):
        rows = slice(ROWS * r, ROWS * r + ROWS)
        high, low = split(filters[r] * TERM[r])
        backward[rows, 0:256] = high
        backward[rows, 256:512] = high
        backward[rows, 512:768] = low
    plane, nz = 9 * wavevectors[0:1, :] + wavevectors[1:2, :], wavevectors[2:3, :]
    nz = jnp.where(plane < 0, -nz, nz)
    plane = jnp.abs(plane)
    code = jnp.where(plane > 0, 40 * (nz + 4) + plane - 1, 359 + jnp.abs(nz)).astype(f32)
    column = jnp.broadcast_to(code, (8, LAYER)).T[:, 0:1]
    lane = lax.broadcasted_iota(jnp.int32, (1, HALF), 1).astype(f32)
    copies = jnp.zeros((8, HALF), f32)
    for first in range(0, LAYER, 64):
        hit = jnp.where(column[first : first + 64] == lane, 1.0, 0.0)
        for k in range(0, 64, 8):
            copies = copies + hit[k : k + 8]
    copies = jnp.sum(copies, 0, keepdims=True)
    value = copies * screened[0:1, :]
    norm = jnp.sum(value * screened[0:1, :], 1, keepdims=True)
    value = value * (FACTOR / jnp.sqrt(norm))
    weights[...] = jnp.concatenate([value, value], 1)


def trig(turns):
    x = (turns - jnp.round(turns)) * math.pi
    y = x * x
    s = x * (1 + y * (-1 / 6 + y * (1 / 120 + y * (-1 / 5040 + y * (1 / 362880 + y * (-1 / 39916800 + y * (1 / 6227020800)))))))
    c = 1 + y * (-1 / 2 + y * (1 / 24 + y * (-1 / 720 + y * (1 / 40320 + y * (-1 / 3628800 + y * (1 / 479001600))))))
    return 1 - 2 * s * s, 2 * s * c


def structure_kernel(packed, cotangent, digits, keep, send, cot_masked, table_high, table_low, sums):
    space = lax.axis_index("space")
    core, x = space % 2, (space // 2) % 4
    row_x = (packed[ROWS : ROWS + 1, :] + space.astype(f32)) * (1 / 64)
    row_y = packed[ROWS + 1 : ROWS + 2, :] * 0.5
    row_z = packed[ROWS + 2 : ROWS + 3, :]

    def put(at, cos, sin):
        for base, value in ((at, cos), (HALF + at, sin)):
            high, low = split(value)
            table_high[base : base + value.shape[0], :] = high
            table_low[base : base + value.shape[0], :] = low

    tall = lax.broadcasted_iota(jnp.int32, (24, 1), 0).astype(f32) + 1.0
    cos_z, sin_z = trig(tall * row_z)
    put(360, cos_z, sin_z)
    cos_p, sin_p = trig(digits[0:40, 0:1] * row_x + digits[0:40, 1:2] * row_y)
    put(160, cos_p, sin_p)
    for n in range(1, 5):
        c, s = cos_z[n - 1 : n, :], sin_z[n - 1 : n, :]
        cc, ss, sc, cs = cos_p * c, sin_p * s, sin_p * c, cos_p * s
        put(160 + 40 * n, cc - ss, sc + cs)
        put(160 - 40 * n, cc + ss, sc - cs)
    masked_high, masked_low = split(packed[0:ROWS, :])
    cot = cotangent[...] * packed[ROWS + 3 : ROWS + 4, :]
    cot_masked[...] = cot
    cot_high, cot_low = split(cot)
    fields = jnp.concatenate([masked_high, cot_high, masked_low, cot_low], 0)
    both = dot(fields, table_high[...], NT) + dot(fields, table_low[...], NT)
    sums[...] = both[:128] + both[128:]
    for d in range(4):
        rows = slice(16 * d, 16 * d + 16)
        place = 16 * jnp.bitwise_xor(x, d)
        keep[rows, :] = sums[pl.ds(pl.multiple_of(core * ROWS + place, 16), 16), :]
        send[rows, :] = sums[pl.ds(pl.multiple_of((1 - core) * ROWS + place, 16), 16), :]


def radial_terms(col, row):
    dx, dy, dz = (col[a] - row[a] for a in range(3))
    square = jnp.minimum(dx * dx + dy * dy + dz * dz, SCALE * SCALE)
    inside = SCALE * SCALE - square
    u = square * lax.rsqrt(jnp.maximum(square, 1e-20)) - 4.0 * LOG2E
    bend = u * (0.5 / LOG2E)
    base = inside * inside
    up, down = jnp.exp2(u), jnp.exp2(-u)
    terms = [None] * NRAD
    terms[4] = base * jnp.exp2(u * (0.5 - bend))
    terms[3] = base * jnp.exp2(u * (-0.5 - bend))
    for k in range(3):
        terms[5 + k] = terms[4 + k] * up
        terms[2 - k] = terms[3 - k] * down
    return terms


def store_terms(tiles, col, row):
    for r, term in enumerate(radial_terms(col, row)):
        high, low = split(term)
        tiles[256 * r : 256 * r + 128, :] = high
        tiles[256 * r + 128 : 256 * r + 256, :] = low


def count_live(sources, amounts):
    for section, source in enumerate(sources):
        for side in range(2):
            lanes = slice(side * CAP, (side + 1) * CAP)
            amounts[2 * section + side] = jnp.sum(source[ROWS + 3 : ROWS + 4, lanes]).astype(jnp.int32)


def list_live(block, neighbours, amounts, pieces):
    def gather(index, found):
        chosen, side = neighbours[block, index // 2], index % 2
        pieces[found] = 2 * chosen + side
        return found + jnp.where(side * 128 < amounts[chosen], 1, 0)

    found = lax.fori_loop(0, 2 * NB, gather, jnp.int32(0))
    pieces[found] = 12
    return found


def forward_setup(sources, places, values):
    for section, source in enumerate(sources):
        at = slice(section * LAYER, (section + 1) * LAYER)
        flipped = source[ROWS:PACK, :].T * SCALE
        lane = lax.broadcasted_iota(jnp.int32, (LAYER, 8), 1)
        places[at, :] = flipped + jnp.where(lane == 0, (section - 1.0) * SCALE, 0.0)
        high, low = split(source[0:ROWS, :])
        for side in range(4):
            values[4 * section + side, 0:ROWS, :] = high[:, 128 * side : 128 * side + 128]
            values[4 * section + side, ROWS:128, :] = low[:, 128 * side : 128 * side + 128]
    places[3 * LAYER :, :] = jnp.zeros((128, 8), f32)


def forward_block(block, neighbours, sources, filters, out, places, values,
                  amounts, pieces, columns, left, right, sums):
    own = sources[1]
    count_live(sources, amounts)
    sums[...] = jnp.zeros_like(sums)
    lines = [
        [own[ROWS + a : ROWS + a + 1, block * CAP + 128 * k : block * CAP + 128 * k + 128] * SCALE for a in range(3)]
        for k in range(2)
    ]
    found = list_live(block, neighbours, amounts, pieces)

    def spread(piece):
        at = pl.ds(pl.multiple_of(piece * 128, 128), 128)
        for a in range(3):
            columns[a] = jnp.broadcast_to(places[at, a : a + 1], (128, 128))

    def flush(piece):
        value = values[piece]
        value = jnp.concatenate([value, value], 1)
        for r in range(NRAD):
            rows = slice(256 * r, 256 * r + 256)
            at = slice(128 * r, 128 * r + 128)
            sums[at, :] = sums[at, :] + dot(value, jnp.concatenate([left[rows, :], right[rows, :]], 1))

    def fill(index):
        col = [columns[a] for a in range(3)]
        for tiles, line in ((left, lines[0]), (right, lines[1])):
            store_terms(tiles, col, line)
        spread(pieces[index + 1])
        return pieces[index]

    def step(index, last):
        flush(last)
        return fill(index)

    spread(pieces[0])
    flush(lax.fori_loop(1, found, step, fill(0)))
    first, second = [], []
    for r in range(NRAD):
        high, low = split(sums[128 * r : 128 * r + ROWS, :] + sums[128 * r + ROWS : 128 * r + 128, :])
        first.append(high)
        second.append(low)
    out[...] = dot(filters[...], jnp.concatenate([*first, *first, *second], 0))


def forward_first_kernel(neighbours, own, below, above, filters, share, places, values, *scratch):
    forward_setup((below, own, above), places, values)
    forward_block(0, neighbours, (below, own, above), filters, share, places, values, *scratch)


def forward_second_kernel(neighbours, own, below, above, filters, other, places, values,
                          own_panel, third_panel, near_panel, far_panel, share, *scratch):
    mine = lax.axis_index("chan")
    forward_block(1, neighbours, (below, own, above), filters, share, places, values, *scratch)
    for out, flip in ((own_panel, 0), (third_panel, 3), (near_panel, 1), (far_panel, 2)):
        rows = pl.ds(pl.multiple_of(ROWS * jnp.bitwise_xor(mine, flip), ROWS), ROWS)
        out[:, 0:CAP] = other[rows, :]
        out[:, CAP:LAYER] = share[rows, :]


def activation_kernel(own_panel, near, third, cot_masked, activated, upstream):
    pre = own_panel[...] + near[...] + third[...]
    sigma = 1.0 / (1.0 + jnp.exp(-pre))
    activated[...] = pre * sigma
    upstream[...] = cot_masked[...] * (sigma * (1.0 + pre * (1.0 - sigma)))


def backward_kernel(neighbours, own, below, above, filters, mine_up, third_up, near_up, far_up,
                    low_side, middle, high_side, columns, lines, amounts, pieces, panels, cots, left, right, sums):
    mine = lax.axis_index("chan")
    sources = (below, own, above)
    count_live(sources, amounts)
    ups = [mine_up[...], third_up[...], near_up[...], far_up[...]]
    for value, flip in zip(ups, (0, 3, 1, 2)):
        first, second = split(value)
        at = ROWS * jnp.bitwise_xor(mine, flip)
        panels[pl.ds(pl.multiple_of(at, ROWS), ROWS), :] = first
        panels[pl.ds(pl.multiple_of(at + 256, ROWS), ROWS), :] = second
        panels[pl.ds(pl.multiple_of(at + 512, ROWS), ROWS), :] = first
    flipped = own[ROWS:PACK, :].T * SCALE
    for a in range(3):
        columns[a] = jnp.broadcast_to(flipped[:, a : a + 1], (LAYER, 128))
    for section, source in enumerate(sources):
        for side in range(4):
            for a in range(3):
                at = slice(ROWS + a, ROWS + a + 1)
                shift = (section - 1.0) * SCALE if a == 0 else 0.0
                lines[4 * section + side, a : a + 1, :] = source[at, 128 * side : 128 * side + 128] * SCALE + shift
    lines[12] = jnp.full((8, 128), 1e4, f32)
    cot = dot(filters[...], panels[...])
    for r in range(NRAD):
        first, second = split(cot[ROWS * r : ROWS * r + ROWS])
        for where in range(4):
            cots[NRAD * where + r, 0:ROWS, :] = first[:, 128 * where : 128 * where + 128]
            cots[NRAD * where + r, ROWS:128, :] = second[:, 128 * where : 128 * where + 128]
    sums[...] = jnp.zeros_like(sums)

    def flush(where, one, two):
        parts = []
        for r in range(NRAD):
            parts += [cots[NRAD * where + r]] * 2
        out = dot(jnp.concatenate(parts, 1), jnp.concatenate([left[...], right[...]], 1))
        for piece, lanes in ((one, slice(0, 128)), (two, slice(128, 256))):
            rows = pl.ds(pl.multiple_of(piece * 128, 128), 128)
            sums[rows, :] = sums[rows, :] + out[:, lanes]

    def fill(where, one, two):
        at = pl.ds(pl.multiple_of(where * 128, 128), 128)
        col = [columns[a, at, :] for a in range(3)]
        for tiles, piece in ((left, one), (right, two)):
            store_terms(tiles, col, [lines[piece, a : a + 1, :] for a in range(3)])
        return where, one, two

    carry = None
    for block in range(2):
        found = list_live(block, neighbours, amounts, pieces)
        pairs = (found + 1) // 2
        total = pairs * ((amounts[2 + block] + 127) // 128)
        if block == 0:
            carry = fill(jnp.int32(0), pieces[0], pieces[1])

        def step(index, last):
            flush(*last)
            half = jnp.where(index >= pairs, 1, 0)
            pair = index - half * pairs
            return fill(2 * block + half, pieces[2 * pair], pieces[2 * pair + 1])

        carry = lax.fori_loop(1 - block, total, step, carry)
    flush(*carry)
    for section, out in enumerate((low_side, middle, high_side)):
        for side in range(4):
            at = 128 * (4 * section + side)
            out[:, 128 * side : 128 * side + 128] = sums[at : at + ROWS, :] + sums[at + ROWS : at + 128, :]


def project_kernel(mine, one, two, three, weights, table_high, table_low, packed, activated, cot_masked, middle,
                   updated, partial, scratch):
    space = lax.axis_index("space")
    core, x = space % 2, (space // 2) % 4
    for d, piece in enumerate((mine, one, two, three)):
        first, second = split(piece[...] * weights[...])
        for half, at in ((0, core), (1, 1 - core)):
            rows = slice(16 * half, 16 * half + 16)
            place = at * ROWS + 16 * jnp.bitwise_xor(x, d)
            scratch[pl.ds(pl.multiple_of(place, 16), 16), :] = first[rows]
            scratch[pl.ds(pl.multiple_of(place + 128, 16), 16), :] = second[rows]
    both = dot(scratch[...], table_high[...]) + dot(scratch[...], table_low[...])
    live = packed[ROWS + 3 : ROWS + 4, :]
    updated[...] = live * (packed[0:ROWS, :] + activated[...] + (both[:ROWS] + both[128 : 128 + ROWS]))
    partial[...] = live * (cot_masked[...] + middle[...] + (both[ROWS:128] + both[128 + ROWS :]))


def screening():
    nx, ny, nz = half_space()
    qx, qy, qz = 2 * math.pi / 64 * nx, math.pi * ny, 2 * math.pi * nz
    square = qx * qx + qy * qy + qz * qz
    return np.tile((np.exp(-square / 2000.0) / (square + 100.0)).astype(np.float32), (8, 1))


def shards(features, positions, counts, neighbours, wavevectors, filters, cotangent):
    n_space = lax.axis_size("space")

    def shift(v, d):
        return lax.ppermute(v, "space", [(i, (i + d) % n_space) for i in range(n_space)])

    def swap(v, mask):
        return lax.ppermute(v, "space", [(i, i ^ mask) for i in range(n_space)])

    def chan_swap(v, mask):
        return lax.ppermute(v, "chan", [(i, i ^ mask) for i in range(4)])

    packed = call(pack_kernel, shape(PACK, LAYER), 1, 2, far=(1, 2))(counts, features, positions)
    below = shift(packed, 1)
    above = shift(packed, -1)

    digits = np.zeros((HALF, 8), np.float32)
    digits[:, :3] = np.stack(half_space(), 1)
    keep, send, cot_masked, table_high, table_low = call(
        structure_kernel,
        (shape(ROWS, 768), shape(ROWS, 768), shape(ROWS, LAYER),
         shape(768, LAYER, dtype=bf16), shape(768, LAYER, dtype=bf16)),
        0, 3, [pltpu.VMEM((128, 768), f32)], far=(1, 2),
    )(packed, cotangent, jnp.asarray(digits))
    forward_filters = call(forward_filter_kernel, shape(256, 1536, dtype=bf16), 0, 1, far=(0,))(filters)
    half = keep + swap(send, 1)
    got = []
    for d in (1, 2, 3):
        got.append(swap(half[16 * d : 16 * d + 16], 2 * d))

    scratch = [
        pltpu.SMEM((6,), jnp.int32),
        pltpu.SMEM((10,), jnp.int32),
        pltpu.VMEM((3, 128, 128), f32),
        pltpu.VMEM((2048, 128), bf16),
        pltpu.VMEM((2048, 128), bf16),
        pltpu.VMEM((1024, CAP), f32),
    ]
    share, places, values = call(
        forward_first_kernel,
        (shape(256, CAP), shape(3 * LAYER + 128, 8), shape(12, 128, 128, dtype=bf16)),
        1, 4, scratch,
    )(neighbours, packed, below, above, forward_filters)
    quarter = half[:16] + got[0] + got[1] + got[2]
    quarter = quarter + swap(quarter, 8)
    own_panel, third_panel, near_panel, far_panel = call(
        forward_second_kernel, tuple([shape(ROWS, LAYER)] * 4), 1, 7,
        [pltpu.VMEM((256, CAP), f32), *scratch],
    )(neighbours, packed, below, above, forward_filters, share, places, values)
    far = chan_swap(far_panel, 1)
    near = chan_swap(near_panel, 1)
    quarter = quarter + swap(quarter, 32)
    third_panel = third_panel + far
    third = chan_swap(third_panel, 3)
    quarter = quarter + swap(quarter, 16)
    backward_filters, weights = call(
        backward_filter_kernel, (shape(512, 768, dtype=bf16), shape(1, 768)), 0, 3,
        far=(0, 1, 2),
    )(filters, wavevectors, jnp.asarray(screening()))
    activated, upstream = call(
        activation_kernel, (shape(ROWS, LAYER), shape(ROWS, LAYER)), 0, 4
    )(own_panel, near, third, cot_masked)
    third_up = chan_swap(upstream, 3)
    near_up = chan_swap(upstream, 1)
    far_up = chan_swap(third_up, 1)
    pair = jnp.concatenate([quarter, swap(quarter, 1)], 0)
    got = []
    for d in (1, 2, 3):
        got.append(swap(pair, 2 * d))
    left, middle, right = call(
        backward_kernel, tuple([shape(ROWS, LAYER)] * 3), 1, 8,
        [
            pltpu.VMEM((3, LAYER, 128), f32),
            pltpu.VMEM((13, 8, 128), f32),
            pltpu.SMEM((6,), jnp.int32),
            pltpu.SMEM((10,), jnp.int32),
            pltpu.VMEM((768, LAYER), bf16),
            pltpu.VMEM((32, 128, 128), bf16),
            pltpu.VMEM((2048, 128), bf16),
            pltpu.VMEM((2048, 128), bf16),
            pltpu.VMEM((13 * 128, 128), f32),
        ],
    )(neighbours, packed, below, above, backward_filters, upstream, third_up, near_up, far_up)
    from_lower = shift(right, 1)
    from_upper = shift(left, -1)
    updated, partial = call(
        project_kernel, (jax.ShapeDtypeStruct((ROWS, LAYER), f32), shape(ROWS, LAYER)), 0, 11,
        [pltpu.VMEM((256, 768), bf16)],
    )(pair, *got, weights, table_high, table_low, packed, activated, cot_masked, middle)
    grad_features = partial + packed[ROWS + 3][None] * (from_lower + from_upper)
    return updated, grad_features


def solution(mesh):
    return jax.shard_map(
        shards,
        mesh=mesh,
        in_specs=(
            P("chan", "space"),
            P(None, "space"),
            P("space"),
            P("space", None),
            P(),
            P(None, "chan", None),
            P("chan", "space"),
        ),
        out_specs=(P("chan", "space"), P("chan", "space")),
        check_vma=False,
    )
```

```python
import math

import jax
import jax.numpy as jnp
import numpy as np
from jax import lax
from jax.experimental import pallas as pl
from jax.experimental.pallas import tpu as pltpu
from jax.sharding import PartitionSpec as P

NRAD = 8
NB = 4
CAP = 256
LAYER = 512
HALF = 384
ROWS = 64
PACK = 72
FACTOR = math.sqrt(3.0 / 32768.0)
LOG2E = math.log2(math.e)
SCALE = 8.0 * LOG2E
TERM = [0.3 * math.exp(-0.5 * (r - 3.5) ** 2) / SCALE**4 for r in range(NRAD)]
VMEM_BYTES = 24 << 20


vmem = pl.BlockSpec(memory_space=pltpu.VMEM)
smem = pl.BlockSpec(memory_space=pltpu.SMEM)
f32, bf16 = jnp.float32, jnp.bfloat16
NT = (((1,), (1,)), ((), ()))
NN = (((1,), (0,)), ((), ()))


def half_space():
    m = np.arange(HALF)
    plane = np.where(m < 360, m % 40 + 1, 0)
    ny = (plane + 4) % 9 - 4
    nx = (plane - ny) // 9
    nz = np.where(m < 360, m // 40 - 4, m - 359)
    return nx, ny, nz


def dot(a, b, dims=NN):
    return lax.dot_general(a, b, dims, preferred_element_type=f32)


def split(value):
    high = value.astype(bf16)
    return high, (value - high.astype(f32)).astype(bf16)


def shape(*dims, dtype=f32):
    return pltpu.VMEM(dims, dtype)


def call(kernel, out, n_smem, n_vmem, scratch=(), far=()):
    many = isinstance(out, tuple)
    run = pl.pallas_call(
        kernel,
        out_shape=out,
        in_specs=[smem] * n_smem + [vmem] * n_vmem,
        out_specs=tuple([vmem] * len(out)) if many else vmem,
        scratch_shapes=list(scratch),
        compiler_params=pltpu.CompilerParams(vmem_limit_bytes=VMEM_BYTES),
    )

    def place(*operands):
        put = pltpu.with_memory_space_constraint
        return run(
            *[put(v, pltpu.HBM if k < n_smem or k in far else pltpu.VMEM) for k, v in enumerate(operands)]
        )

    return place


def live_row(counts):
    lane = lax.broadcasted_iota(jnp.int32, (1, LAYER), 1)
    bound = jnp.where(lane < CAP, counts[0], counts[1] + CAP)
    return (lane < bound).astype(f32)


def pack_kernel(counts, features, positions, cotangent, packed, cot_masked):
    live = live_row(counts)
    packed[0:ROWS, :] = features[...] * live
    packed[ROWS : ROWS + 3, :] = positions[...]
    packed[ROWS + 3 : PACK, :] = jnp.broadcast_to(live, (PACK - ROWS - 3, LAYER))
    cot_masked[...] = cotangent[...] * live


def forward_filter_kernel(filters, forward):
    scaled = jnp.concatenate([filters[r] * TERM[r] for r in range(NRAD)], 0)
    high, low = split(scaled.T)
    forward[:, 0:512] = high
    forward[:, 512:1024] = low
    forward[:, 1024:1536] = high


def backward_filter_kernel(filters, wavevectors, screened, own, below, above, backward, weights, columns, lines):
    for r in range(NRAD):
        rows = slice(ROWS * r, ROWS * r + ROWS)
        high, low = split(filters[r] * TERM[r])
        backward[rows, 0:256] = high
        backward[rows, 256:512] = high
        backward[rows, 512:768] = low
    plane, nz = 9 * wavevectors[0:1, :] + wavevectors[1:2, :], wavevectors[2:3, :]
    nz = jnp.where(plane < 0, -nz, nz)
    plane = jnp.abs(plane)
    code = jnp.where(plane > 0, 40 * (nz + 4) + plane - 1, 359 + jnp.abs(nz)).astype(f32)
    column = jnp.broadcast_to(code, (8, LAYER)).T[:, 0:1]
    lane = lax.broadcasted_iota(jnp.int32, (1, HALF), 1).astype(f32)
    copies = jnp.zeros((8, HALF), f32)
    for first in range(0, LAYER, 64):
        hit = jnp.where(column[first : first + 64] == lane, 1.0, 0.0)
        for k in range(0, 64, 8):
            copies = copies + hit[k : k + 8]
    copies = jnp.sum(copies, 0, keepdims=True)
    value = copies * screened[0:1, :]
    norm = jnp.sum(value * screened[0:1, :], 1, keepdims=True)
    value = value * (FACTOR / jnp.sqrt(norm))
    weights[...] = jnp.concatenate([value, value], 1)
    flipped = own[ROWS:PACK, :].T * SCALE
    for a in range(3):
        columns[a] = jnp.broadcast_to(flipped[:, a : a + 1], (LAYER, 128))
    for section, source in enumerate((below, own, above)):
        for side in range(4):
            for a in range(3):
                at = slice(ROWS + a, ROWS + a + 1)
                shift = (section - 1.0) * SCALE if a == 0 else 0.0
                lines[4 * section + side, a : a + 1, :] = source[at, 128 * side : 128 * side + 128] * SCALE + shift
    lines[12] = jnp.full((8, 128), 1e4, f32)


def trig(turns):
    x = (turns - jnp.round(turns)) * math.pi
    y = x * x
    s = x * (1 + y * (-1 / 6 + y * (1 / 120 + y * (-1 / 5040 + y * (1 / 362880 + y * (-1 / 39916800 + y * (1 / 6227020800)))))))
    c = 1 + y * (-1 / 2 + y * (1 / 24 + y * (-1 / 720 + y * (1 / 40320 + y * (-1 / 3628800 + y * (1 / 479001600))))))
    return 1 - 2 * s * s, 2 * s * c


def structure_kernel(packed, cot_masked, digits, keep, send, table_high, table_low, sums):
    space = lax.axis_index("space")
    core, x = space % 2, (space // 2) % 4
    row_x = (packed[ROWS : ROWS + 1, :] + space.astype(f32)) * (1 / 64)
    row_y = packed[ROWS + 1 : ROWS + 2, :] * 0.5
    row_z = packed[ROWS + 2 : ROWS + 3, :]

    def put(at, cos, sin):
        for base, value in ((at, cos), (HALF + at, sin)):
            high, low = split(value)
            table_high[base : base + value.shape[0], :] = high
            table_low[base : base + value.shape[0], :] = low

    tall = lax.broadcasted_iota(jnp.int32, (24, 1), 0).astype(f32) + 1.0
    cos_z, sin_z = trig(tall * row_z)
    put(360, cos_z, sin_z)
    cos_p, sin_p = trig(digits[0:40, 0:1] * row_x + digits[0:40, 1:2] * row_y)
    put(160, cos_p, sin_p)
    for n in range(1, 5):
        c, s = cos_z[n - 1 : n, :], sin_z[n - 1 : n, :]
        cc, ss, sc, cs = cos_p * c, sin_p * s, sin_p * c, cos_p * s
        put(160 + 40 * n, cc - ss, sc + cs)
        put(160 - 40 * n, cc + ss, sc - cs)
    masked_high, masked_low = split(packed[0:ROWS, :])
    cot_high, cot_low = split(cot_masked[...])
    fields = jnp.concatenate([masked_high, cot_high, masked_low, cot_low], 0)
    both = dot(fields, table_high[...], NT) + dot(fields, table_low[...], NT)
    sums[...] = both[:128] + both[128:]
    for d in range(4):
        rows = slice(16 * d, 16 * d + 16)
        place = 16 * jnp.bitwise_xor(x, d)
        keep[rows, :] = sums[pl.ds(pl.multiple_of(core * ROWS + place, 16), 16), :]
        send[rows, :] = sums[pl.ds(pl.multiple_of((1 - core) * ROWS + place, 16), 16), :]


def radial_terms(col, row):
    dx, dy, dz = (col[a] - row[a] for a in range(3))
    square = jnp.minimum(dx * dx + dy * dy + dz * dz, SCALE * SCALE)
    inside = SCALE * SCALE - square
    u = square * lax.rsqrt(jnp.maximum(square, 1e-20)) - 4.0 * LOG2E
    bend = u * (0.5 / LOG2E)
    base = inside * inside
    up, down = jnp.exp2(u), jnp.exp2(-u)
    terms = [None] * NRAD
    terms[4] = base * jnp.exp2(u * (0.5 - bend))
    terms[3] = base * jnp.exp2(u * (-0.5 - bend))
    for k in range(3):
        terms[5 + k] = terms[4 + k] * up
        terms[2 - k] = terms[3 - k] * down
    return terms


def store_terms(tiles, col, row):
    for r, term in enumerate(radial_terms(col, row)):
        high, low = split(term)
        tiles[256 * r : 256 * r + 128, :] = high
        tiles[256 * r + 128 : 256 * r + 256, :] = low


def count_live(sources, amounts):
    for section, source in enumerate(sources):
        for side in range(2):
            lanes = slice(side * CAP, (side + 1) * CAP)
            amounts[2 * section + side] = jnp.sum(source[ROWS + 3 : ROWS + 4, lanes]).astype(jnp.int32)


def list_live(block, neighbours, amounts, pieces):
    def gather(index, found):
        chosen, side = neighbours[block, index // 2], index % 2
        pieces[found] = 2 * chosen + side
        return found + jnp.where(side * 128 < amounts[chosen], 1, 0)

    found = lax.fori_loop(0, 2 * NB, gather, jnp.int32(0))
    pieces[found] = 12
    return found


def forward_setup(sources, places, values):
    for section, source in enumerate(sources):
        at = slice(section * LAYER, (section + 1) * LAYER)
        flipped = source[ROWS:PACK, :].T * SCALE
        lane = lax.broadcasted_iota(jnp.int32, (LAYER, 8), 1)
        places[at, :] = flipped + jnp.where(lane == 0, (section - 1.0) * SCALE, 0.0)
        high, low = split(source[0:ROWS, :])
        for side in range(4):
            values[4 * section + side, 0:ROWS, :] = high[:, 128 * side : 128 * side + 128]
            values[4 * section + side, ROWS:128, :] = low[:, 128 * side : 128 * side + 128]
    places[3 * LAYER :, :] = jnp.zeros((128, 8), f32)


def forward_block(block, neighbours, sources, filters, out, places, values,
                  amounts, pieces, columns, left, right, sums):
    own = sources[1]
    count_live(sources, amounts)
    sums[...] = jnp.zeros_like(sums)
    lines = [
        [own[ROWS + a : ROWS + a + 1, block * CAP + 128 * k : block * CAP + 128 * k + 128] * SCALE for a in range(3)]
        for k in range(2)
    ]
    found = list_live(block, neighbours, amounts, pieces)

    def spread(piece):
        at = pl.ds(pl.multiple_of(piece * 128, 128), 128)
        for a in range(3):
            columns[a] = jnp.broadcast_to(places[at, a : a + 1], (128, 128))

    def flush(piece):
        value = values[piece]
        value = jnp.concatenate([value, value], 1)
        for r in range(NRAD):
            rows = slice(256 * r, 256 * r + 256)
            at = slice(128 * r, 128 * r + 128)
            sums[at, :] = sums[at, :] + dot(value, jnp.concatenate([left[rows, :], right[rows, :]], 1))

    def fill(index):
        col = [columns[a] for a in range(3)]
        for tiles, line in ((left, lines[0]), (right, lines[1])):
            store_terms(tiles, col, line)
        spread(pieces[index + 1])
        return pieces[index]

    def step(index, last):
        flush(last)
        return fill(index)

    spread(pieces[0])
    flush(lax.fori_loop(1, found, step, fill(0)))
    first, second = [], []
    for r in range(NRAD):
        high, low = split(sums[128 * r : 128 * r + ROWS, :] + sums[128 * r + ROWS : 128 * r + 128, :])
        first.append(high)
        second.append(low)
    out[...] = dot(filters[...], jnp.concatenate([*first, *first, *second], 0))


def forward_first_kernel(neighbours, own, below, above, filters, share, places, values, *scratch):
    forward_setup((below, own, above), places, values)
    forward_block(0, neighbours, (below, own, above), filters, share, places, values, *scratch)


def forward_second_kernel(neighbours, own, below, above, filters, other, places, values,
                          own_panel, third_panel, near_panel, far_panel, share, *scratch):
    mine = lax.axis_index("chan")
    forward_block(1, neighbours, (below, own, above), filters, share, places, values, *scratch)
    for out, flip in ((own_panel, 0), (third_panel, 3), (near_panel, 1), (far_panel, 2)):
        rows = pl.ds(pl.multiple_of(ROWS * jnp.bitwise_xor(mine, flip), ROWS), ROWS)
        out[:, 0:CAP] = other[rows, :]
        out[:, CAP:LAYER] = share[rows, :]


def activation_kernel(own_panel, near, third, cot_masked, activated, upstream):
    pre = own_panel[...] + near[...] + third[...]
    sigma = 1.0 / (1.0 + jnp.exp(-pre))
    activated[...] = pre * sigma
    upstream[...] = cot_masked[...] * (sigma * (1.0 + pre * (1.0 - sigma)))


def backward_kernel(neighbours, own, below, above, filters, columns, lines, mine_up, third_up, near_up, far_up,
                    low_side, middle, high_side, amounts, pieces, panels, cots, left, right, sums):
    mine = lax.axis_index("chan")
    sources = (below, own, above)
    count_live(sources, amounts)
    ups = [mine_up[...], third_up[...], near_up[...], far_up[...]]
    for value, flip in zip(ups, (0, 3, 1, 2)):
        first, second = split(value)
        at = ROWS * jnp.bitwise_xor(mine, flip)
        panels[pl.ds(pl.multiple_of(at, ROWS), ROWS), :] = first
        panels[pl.ds(pl.multiple_of(at + 256, ROWS), ROWS), :] = second
        panels[pl.ds(pl.multiple_of(at + 512, ROWS), ROWS), :] = first
    cot = dot(filters[...], panels[...])
    for r in range(NRAD):
        first, second = split(cot[ROWS * r : ROWS * r + ROWS])
        for where in range(4):
            cots[NRAD * where + r, 0:ROWS, :] = first[:, 128 * where : 128 * where + 128]
            cots[NRAD * where + r, ROWS:128, :] = second[:, 128 * where : 128 * where + 128]
    sums[...] = jnp.zeros_like(sums)

    def flush(where, one, two):
        parts = []
        for r in range(NRAD):
            parts += [cots[NRAD * where + r]] * 2
        out = dot(jnp.concatenate(parts, 1), jnp.concatenate([left[...], right[...]], 1))
        for piece, lanes in ((one, slice(0, 128)), (two, slice(128, 256))):
            rows = pl.ds(pl.multiple_of(piece * 128, 128), 128)
            sums[rows, :] = sums[rows, :] + out[:, lanes]

    def fill(where, one, two):
        at = pl.ds(pl.multiple_of(where * 128, 128), 128)
        col = [columns[a, at, :] for a in range(3)]
        for tiles, piece in ((left, one), (right, two)):
            store_terms(tiles, col, [lines[piece, a : a + 1, :] for a in range(3)])
        return where, one, two

    carry = None
    for block in range(2):
        found = list_live(block, neighbours, amounts, pieces)
        pairs = (found + 1) // 2
        total = pairs * ((amounts[2 + block] + 127) // 128)
        if block == 0:
            carry = fill(jnp.int32(0), pieces[0], pieces[1])

        def step(index, last):
            flush(*last)
            half = jnp.where(index >= pairs, 1, 0)
            pair = index - half * pairs
            return fill(2 * block + half, pieces[2 * pair], pieces[2 * pair + 1])

        carry = lax.fori_loop(1 - block, total, step, carry)
    flush(*carry)
    for section, out in enumerate((low_side, middle, high_side)):
        for side in range(4):
            at = 128 * (4 * section + side)
            out[:, 128 * side : 128 * side + 128] = sums[at : at + ROWS, :] + sums[at + ROWS : at + 128, :]


def project_kernel(mine, one, two, three, weights, table_high, table_low, packed, activated, cot_masked, middle,
                   updated, partial, scratch):
    space = lax.axis_index("space")
    core, x = space % 2, (space // 2) % 4
    for d, piece in enumerate((mine, one, two, three)):
        first, second = split(piece[...] * weights[...])
        for half, at in ((0, core), (1, 1 - core)):
            rows = slice(16 * half, 16 * half + 16)
            place = at * ROWS + 16 * jnp.bitwise_xor(x, d)
            scratch[pl.ds(pl.multiple_of(place, 16), 16), :] = first[rows]
            scratch[pl.ds(pl.multiple_of(place + 128, 16), 16), :] = second[rows]
    both = dot(scratch[...], table_high[...]) + dot(scratch[...], table_low[...])
    live = packed[ROWS + 3 : ROWS + 4, :]
    updated[...] = live * (packed[0:ROWS, :] + activated[...] + (both[:ROWS] + both[128 : 128 + ROWS]))
    partial[...] = live * (cot_masked[...] + middle[...] + (both[ROWS:128] + both[128 + ROWS :]))


def screening():
    nx, ny, nz = half_space()
    qx, qy, qz = 2 * math.pi / 64 * nx, math.pi * ny, 2 * math.pi * nz
    square = qx * qx + qy * qy + qz * qz
    return np.tile((np.exp(-square / 2000.0) / (square + 100.0)).astype(np.float32), (8, 1))


def shards(features, positions, counts, neighbours, wavevectors, filters, cotangent):
    n_space = lax.axis_size("space")

    def shift(v, d):
        return lax.ppermute(v, "space", [(i, (i + d) % n_space) for i in range(n_space)])

    def swap(v, mask):
        return lax.ppermute(v, "space", [(i, i ^ mask) for i in range(n_space)])

    def chan_swap(v, mask):
        return lax.ppermute(v, "chan", [(i, i ^ mask) for i in range(4)])

    packed, cot_masked = call(
        pack_kernel, (shape(PACK, LAYER), shape(ROWS, LAYER)), 1, 3, far=(1, 2, 3)
    )(counts, features, positions, cotangent)
    below = shift(packed, 1)
    above = shift(packed, -1)

    digits = np.zeros((HALF, 8), np.float32)
    digits[:, :3] = np.stack(half_space(), 1)
    keep, send, table_high, table_low = call(
        structure_kernel,
        (shape(ROWS, 768), shape(ROWS, 768),
         shape(768, LAYER, dtype=bf16), shape(768, LAYER, dtype=bf16)),
        0, 3, [pltpu.VMEM((128, 768), f32)], far=(2,),
    )(packed, cot_masked, jnp.asarray(digits[:40]))
    forward_filters = call(forward_filter_kernel, shape(256, 1536, dtype=bf16), 0, 1, far=(0,))(filters)
    half = keep + swap(send, 1)
    got = []
    for d in (1, 2, 3):
        got.append(swap(half[16 * d : 16 * d + 16], 2 * d))

    scratch = [
        pltpu.SMEM((6,), jnp.int32),
        pltpu.SMEM((10,), jnp.int32),
        pltpu.VMEM((3, 128, 128), f32),
        pltpu.VMEM((2048, 128), bf16),
        pltpu.VMEM((2048, 128), bf16),
        pltpu.VMEM((1024, CAP), f32),
    ]
    share, places, values = call(
        forward_first_kernel,
        (shape(256, CAP), shape(3 * LAYER + 128, 8), shape(12, 128, 128, dtype=bf16)),
        1, 4, scratch,
    )(neighbours, packed, below, above, forward_filters)
    quarter = half[:16] + got[0] + got[1] + got[2]
    quarter = quarter + swap(quarter, 8)
    own_panel, third_panel, near_panel, far_panel = call(
        forward_second_kernel, tuple([shape(ROWS, LAYER)] * 4), 1, 7,
        [pltpu.VMEM((256, CAP), f32), *scratch],
    )(neighbours, packed, below, above, forward_filters, share, places, values)
    far = chan_swap(far_panel, 1)
    near = chan_swap(near_panel, 1)
    quarter = quarter + swap(quarter, 32)
    third_panel = third_panel + far
    third = chan_swap(third_panel, 3)
    quarter = quarter + swap(quarter, 16)
    backward_filters, weights, columns, lines = call(
        backward_filter_kernel,
        (shape(512, 768, dtype=bf16), shape(1, 768), shape(3, LAYER, 128), shape(13, 8, 128)),
        0, 6, far=(0, 1, 2),
    )(filters, wavevectors, jnp.asarray(screening()), packed, below, above)
    activated, upstream = call(
        activation_kernel, (shape(ROWS, LAYER), shape(ROWS, LAYER)), 0, 4
    )(own_panel, near, third, cot_masked)
    third_up = chan_swap(upstream, 3)
    near_up = chan_swap(upstream, 1)
    far_up = chan_swap(third_up, 1)
    pair = jnp.concatenate([quarter, swap(quarter, 1)], 0)
    got = []
    for d in (1, 2, 3):
        got.append(swap(pair, 2 * d))
    left, middle, right = call(
        backward_kernel, tuple([shape(ROWS, LAYER)] * 3), 1, 10,
        [
            pltpu.SMEM((6,), jnp.int32),
            pltpu.SMEM((10,), jnp.int32),
            pltpu.VMEM((768, LAYER), bf16),
            pltpu.VMEM((32, 128, 128), bf16),
            pltpu.VMEM((2048, 128), bf16),
            pltpu.VMEM((2048, 128), bf16),
            pltpu.VMEM((13 * 128, 128), f32),
        ],
    )(neighbours, packed, below, above, backward_filters, columns, lines,
      upstream, third_up, near_up, far_up)
    from_lower = shift(right, 1)
    from_upper = shift(left, -1)
    updated, partial = call(
        project_kernel, (jax.ShapeDtypeStruct((ROWS, LAYER), f32), shape(ROWS, LAYER)), 0, 11,
        [pltpu.VMEM((256, 768), bf16)],
    )(pair, *got, weights, table_high, table_low, packed, activated, cot_masked, middle)
    grad_features = partial + packed[ROWS + 3][None] * (from_lower + from_upper)
    return updated, grad_features


def solution(mesh):
    return jax.shard_map(
        shards,
        mesh=mesh,
        in_specs=(
            P("chan", "space"),
            P(None, "space"),
            P("space"),
            P("space", None),
            P(),
            P(None, "chan", None),
            P("chan", "space"),
        ),
        out_specs=(P("chan", "space"), P("chan", "space")),
        check_vma=False,
    )
```
